128 devices in a mesh: row: 16 (over y, z), col: 8 (over x, core).
Axes of the slice: x: 4, y: 4, z: 4, core: 2. Of those that a mesh axis runs over, the one named last changes fastest.
Arguments:
- kernel_rows: float32 [2, 16, 8, 64, 16384], P(None, 'row', 'col'), may hold values from -1 to 8, as said below
Outputs:
- factored: float32 [2, 16, 512, 4, 8, 512], P(None, 'row', None, None, 'col')
The draws below stay inside these ranges and needn't reach their ends.
Inputs may be any that keep to these rules, and one draw needn't show every extreme that they name: `kernel_rows`: the matrix A that the rows make is symmetric and positive definite.
All inputs are finite; a program needn't handle non-finite values.
Results may differ from the reference program's by a relative error of at most 0.0001.
Values sent between devices are 32-bit elements; how exact they have to be, the bound alone decides.
A program may use at most 128 MiB of HBM per device.

```python
import math
import jax
import jax.numpy as jnp
from jax import lax

NB = 512
KR = 2
N = 16384
KC = 4
RS = 64
N_ROW = 16
N_COL = 8


def draw_kernel_rows(key, part):
    key_off, key_diag = jax.random.split(key)
    noise = jnp.clip(jax.random.normal(key_off, (N, N), jnp.float32), -4.0, 4.0)
    diagonal = jax.random.uniform(key_diag, (N,), jnp.float32, 4.0, 8.0)
    symmetric = (noise + noise.T) * (1.0 / math.sqrt(N))
    places = jnp.arange(N)
    matrix = jnp.where(places[:, None] == places[None, :], diagonal[:, None], symmetric)
    return matrix.reshape(KR, N_ROW, N_COL, RS, N)


def setup_inputs(seed: int = 0) -> dict:
    streams_of = jax.random.split(jax.random.key(seed), 2)
    kernel_rows = draw_kernel_rows(jax.random.fold_in(streams_of[1], 71), 0)
    return {"kernel_rows": kernel_rows}


def reference(kernel_rows):
    mat_order = kernel_rows.shape[-1]
    matrix = kernel_rows.reshape(mat_order, mat_order)
    for panel_idx in range(2):
        start_at = panel_idx * NB
        end_at = start_at + NB
        factor_tile = jnp.linalg.cholesky(matrix[start_at:end_at, start_at:end_at])
        below_tiles = matrix[end_at:, start_at:end_at]
        solved = jax.scipy.linalg.solve_triangular(factor_tile, below_tiles.T, lower=True).T
        trailing = matrix[end_at:, end_at:] - jnp.dot(solved.astype(jnp.float32), solved.T.astype(jnp.float32), preferred_element_type=jnp.float32, precision=lax.Precision.HIGHEST)
        matrix = matrix.at[end_at:, end_at:].set(trailing)
        matrix = matrix.at[start_at:end_at, start_at:end_at].set(factor_tile)
        matrix = matrix.at[end_at:, start_at:end_at].set(solved)
        matrix = matrix.at[start_at:end_at, end_at:].set(jnp.float32(0.0))
        matrix = matrix.at[:start_at, start_at:end_at].set(jnp.float32(0.0))
    return matrix.reshape(KR, N_ROW, NB, KC, N_COL, NB)
```

```python
import functools
import jax
import jax.numpy as jnp
from jax import lax
from jax.experimental import pallas as pl
from jax.experimental.pallas import tpu as pltpu
from jax.sharding import PartitionSpec as P

MESH = pl.DeviceIdType.MESH
HI = lax.Precision.HIGHEST
F32 = jnp.float32
BF16 = jnp.bfloat16
BLK = 128
STRIP = 8
VMEM_CAP = 64 * 1024 * 1024 - 128 * 1024


def rcopy(src, dst, ssem, rsem, row, col):
    return pltpu.make_async_remote_copy(
        src_ref=src, dst_ref=dst, send_sem=ssem, recv_sem=rsem,
        device_id=(row, col), device_id_type=MESH)


def wait_for(ref, sem):
    pltpu.make_async_copy(ref, ref, sem).wait()


def comm_kernel(kr, tiles, panels, head, slab, own, ssem, rsem, lsem):
    g = lax.axis_index("row")
    c = lax.axis_index("col")
    core = lax.rem(c, 2)
    chip = c // 2
    swap_row = (g // 8) * 8 + c
    swap_col = lax.rem(g, 8)
    is_self = swap_col == c
    slot = 2 + g // 8
    sub = pl.multiple_of(lax.rem(g, 8) * 64, 64)
    mine = pl.multiple_of(c * 64, 64)

    pltpu.make_async_copy(kr.at[:, :, pl.ds(0, 1024)], slab, lsem.at[0]).start()
    for a in range(2):
        for b in range(4):
            at = pl.multiple_of((b * 8 + c) * 512, 512)
            pltpu.make_async_copy(
                kr.at[a, :, pl.ds(at, 512)], own.at[a, b], lsem.at[1]).start()

    barrier = pltpu.get_barrier_semaphore()

    @pl.loop(1, 16)
    def _(o):
        pl.semaphore_signal(barrier, inc=1, device_id=(lax.rem(g + o, 16), c), device_id_type=MESH)

    @pl.loop(1, 8)
    def _(o):
        pl.semaphore_signal(barrier, inc=1, device_id=(g, lax.rem(c + o, 8)), device_id_type=MESH)

    @pl.when(jnp.logical_not(is_self))
    def _():
        pl.semaphore_signal(barrier, inc=1, device_id=(swap_row, swap_col), device_id_type=MESH)
        pl.semaphore_wait(barrier, 23)

    @pl.when(is_self)
    def _():
        pl.semaphore_wait(barrier, 22)

    wait_for(slab, lsem.at[0])

    for a in range(2):
        for o in range(1, 4):
            rcopy(slab.at[a], panels.at[a, pl.ds(mine, 64), :], ssem.at[a], rsem.at[a],
                  g, lax.rem(c + 2 * o, 8)).start()
        rcopy(slab.at[a], panels.at[a, pl.ds(mine, 64), :], ssem.at[2], rsem.at[2],
              g, chip * 2 + 1 - core).start()
        pltpu.make_async_copy(slab.at[a], panels.at[a, pl.ds(mine, 64), :], lsem.at[2]).start()

    @pl.when(jnp.logical_not(is_self))
    def _():
        for a in range(2):
            rcopy(slab.at[a], panels.at[2 + g // 8 + 2 * a, pl.ds(mine, 64), :],
                  ssem.at[3], rsem.at[3], swap_row, swap_col).start()

    @pl.when(is_self)
    def _():
        for a in range(2):
            pltpu.make_async_copy(
                slab.at[a], panels.at[slot + 2 * a, pl.ds(sub, 64), :], lsem.at[3]).start()

    @pl.loop(1, 8)
    def _(o):
        cc = lax.rem(c + o, 8)
        for a in range(2):
            for b in range(4):
                at = pl.multiple_of((b * 8 + cc) * 512, 512)
                rcopy(kr.at[a, :, pl.ds(at, 512)], tiles.at[a, b, pl.ds(mine, 64), :],
                      ssem.at[4], rsem.at[4], g, cc).start()

    wait_for(own, lsem.at[1])
    for a in range(2):
        for b in range(4):
            pltpu.make_async_copy(
                own.at[a, b], tiles.at[a, b, pl.ds(mine, 64), :], lsem.at[4]).start()

    wait_for(panels.at[0, pl.ds(0, 192), :], rsem.at[0])
    wait_for(slab, lsem.at[2])

    def piece_row(q):
        return pl.multiple_of((2 * (q // 4) + core) * 64 + lax.rem(q, 4) * 16, 16)

    def scatter(root, lanes_at, lanes, index):
        @pl.when(g == root)
        def _():
            @pl.loop(1, 16)
            def _(o):
                q = lax.rem(g + o, 16)
                r = piece_row(q)
                rcopy(panels.at[0, pl.ds(r, 16), pl.ds(lanes_at, lanes)],
                      head.at[pl.ds(root * 512 + r, 16), pl.ds(lanes_at, lanes)],
                      ssem.at[5 + index], rsem.at[5 + index], q, c).start()
            r = piece_row(g)
            cp = pltpu.make_async_copy(
                panels.at[0, pl.ds(r, 16), pl.ds(lanes_at, lanes)],
                head.at[pl.ds(root * 512 + r, 16), pl.ds(lanes_at, lanes)], lsem.at[5])
            cp.start()
            cp.wait()

        @pl.when(g != root)
        def _():
            wait_for(head.at[pl.ds(0, 16), pl.ds(lanes_at, lanes)], rsem.at[5 + index])

    def gather(root, lanes_at, lanes, index):
        r = piece_row(g)
        src = head.at[pl.ds(root * 512 + r, 16), pl.ds(lanes_at, lanes)]

        @pl.loop(1, 16)
        def _(o):
            rcopy(src, src, ssem.at[7 + index], rsem.at[7 + index], lax.rem(g + o, 16), c).start()

    def swap(root, lanes_at, lanes, index):
        wait_for(head.at[pl.ds(0, 240), pl.ds(lanes_at, lanes)], rsem.at[7 + index])
        for m in range(4):
            r = pl.multiple_of(root * 512 + (2 * m + core) * 64, 64)
            src = head.at[pl.ds(r, 64), pl.ds(lanes_at, lanes)]
            rcopy(src, src, ssem.at[9 + index], rsem.at[9 + index], g, chip * 2 + 1 - core).start()

    scatter(0, 0, 1024, 0)
    scatter(1, 512, 512, 1)
    gather(0, 0, 1024, 0)
    gather(1, 512, 512, 1)

    @pl.when(jnp.logical_not(is_self))
    def _():
        wait_for(panels.at[0, pl.ds(0, 128), :], rsem.at[3])

    @pl.when(is_self)
    def _():
        wait_for(slab, lsem.at[3])

    @pl.loop(1, 16)
    def _(o):
        q = lax.rem(g + o, 16)
        for a in range(2):
            src = panels.at[slot + 2 * a, pl.ds(sub, 64), :]
            rcopy(src, src, ssem.at[11], rsem.at[11], q, c).start()

    swap(0, 0, 1024, 0)
    swap(1, 512, 512, 1)

    wait_for(panels.at[0, pl.ds(0, 192), :], rsem.at[1])
    for a in range(2):
        for o in range(1, 4):
            at = pl.multiple_of(lax.rem(c + 2 * o, 8) * 64, 64)
            src = panels.at[a, pl.ds(at, 64), :]
            rcopy(src, src, ssem.at[12], rsem.at[12], g, chip * 2 + 1 - core).start()

    wait_for(head.at[pl.ds(0, 256), :], rsem.at[9])
    wait_for(head.at[pl.ds(0, 256), pl.ds(512, 512)], rsem.at[10])
    wait_for(panels.at[0, pl.ds(0, 128), :], rsem.at[2])
    wait_for(panels.at[0, pl.ds(0, 384), :], rsem.at[12])
    wait_for(panels.at[pl.ds(0, 4), pl.ds(0, 480), :], rsem.at[11])
    wait_for(own, lsem.at[4])
    wait_for(tiles.at[:, :, pl.ds(0, 448), :], rsem.at[4])
    wait_for(panels.at[0, pl.ds(0, 192), :], ssem.at[0])
    wait_for(panels.at[0, pl.ds(0, 192), :], ssem.at[1])
    wait_for(panels.at[0, pl.ds(0, 128), :], ssem.at[2])

    @pl.when(jnp.logical_not(is_self))
    def _():
        wait_for(panels.at[0, pl.ds(0, 128), :], ssem.at[3])

    wait_for(tiles.at[:, :, pl.ds(0, 448), :], ssem.at[4])

    @pl.when(g == 0)
    def _():
        wait_for(head.at[pl.ds(0, 240), :], ssem.at[5])

    @pl.when(g == 1)
    def _():
        wait_for(head.at[pl.ds(0, 240), pl.ds(512, 512)], ssem.at[6])

    wait_for(head.at[pl.ds(0, 240), :], ssem.at[7])
    wait_for(head.at[pl.ds(0, 240), pl.ds(512, 512)], ssem.at[8])
    wait_for(head.at[pl.ds(0, 256), :], ssem.at[9])
    wait_for(head.at[pl.ds(0, 256), pl.ds(512, 512)], ssem.at[10])
    wait_for(panels.at[pl.ds(0, 4), pl.ds(0, 480), :], ssem.at[11])
    wait_for(panels.at[0, pl.ds(0, 384), :], ssem.at[12])


def exchange(rows):
    anyspace = pl.BlockSpec(memory_space=pl.ANY)
    return pl.pallas_call(
        comm_kernel,
        out_shape=(
            jax.ShapeDtypeStruct((2, 4, 512, 512), F32),
            jax.ShapeDtypeStruct((6, 512, 1024), F32),
            jax.ShapeDtypeStruct((1024, 1024), F32),
        ),
        in_specs=[anyspace],
        out_specs=(anyspace, anyspace, anyspace),
        scratch_shapes=[
            pltpu.VMEM((2, 64, 1024), F32),
            pltpu.VMEM((2, 4, 64, 512), F32),
            pltpu.SemaphoreType.DMA((13,)),
            pltpu.SemaphoreType.DMA((13,)),
            pltpu.SemaphoreType.DMA((6,)),
        ],
        compiler_params=pltpu.CompilerParams(collective_id=1, has_side_effects=True),
        name="exchange",
    )(rows)


def dot_tn(lhs, rhs):
    return lax.dot_general(lhs, rhs, (((0,), (0,)), ((), ())), precision=HI,
                           preferred_element_type=F32)


def factor_block(block):
    count = BLK // STRIP
    lane = lax.broadcasted_iota(jnp.int32, (STRIP, BLK), 1)
    sublane = lax.broadcasted_iota(jnp.int32, (STRIP, BLK), 0)
    left = [block[STRIP * t:STRIP * (t + 1), :] for t in range(count)]
    right = [jnp.where(lane == sublane + STRIP * t, F32(1.0), F32(0.0)) for t in range(count)]
    upper, inverse = [], []
    for t in range(count):
        row = [jnp.broadcast_to(left[t][i:i + 1, :], (STRIP, BLK)) for i in range(STRIP)]
        inv = [jnp.broadcast_to(right[t][i:i + 1, :], (STRIP, BLK)) for i in range(STRIP)]
        entry = {}
        for i in range(STRIP):
            for j in range(i, STRIP):
                at = STRIP * t + j
                entry[i, j] = jnp.broadcast_to(row[i][:, at:at + 1], (STRIP, BLK))
        for k in range(STRIP):
            scale = lax.rsqrt(entry[k, k])
            row[k] = row[k] * scale
            inv[k] = inv[k] * scale
            factor = {i: entry[k, i] * scale for i in range(k + 1, STRIP)}
            for i in range(k + 1, STRIP):
                for j in range(i, STRIP):
                    entry[i, j] = entry[i, j] - factor[i] * factor[j]
                row[i] = row[i] - factor[i] * row[k]
                inv[i] = inv[i] - factor[i] * inv[k]
        strip_row, strip_inv = row[0], inv[0]
        for i in range(1, STRIP):
            strip_row = jnp.where(sublane == i, row[i], strip_row)
            strip_inv = jnp.where(sublane == i, inv[i], strip_inv)
        strip_row = jnp.where(lane >= sublane + STRIP * t, strip_row, F32(0.0))
        upper.append(strip_row)
        inverse.append(strip_inv)
        if t + 1 < count:
            change = dot_tn(strip_row, jnp.concatenate([strip_row, strip_inv], axis=1))
            for s in range(t + 1, count):
                left[s] = left[s] - change[STRIP * s:STRIP * (s + 1), :BLK]
                right[s] = right[s] - change[STRIP * s:STRIP * (s + 1), BLK:]
    return jnp.concatenate(upper, axis=0), jnp.concatenate(inverse, axis=0)


def factor_kernel(head, lower, winv, work, diag):
    work[...] = head[...]
    blocks = 1024 // BLK
    lane_blk = lax.broadcasted_iota(jnp.int32, (BLK, 1024), 1) // BLK

    @pl.loop(0, blocks)
    def _(kb):
        at = pl.multiple_of(kb * BLK, BLK)
        upper, inverse = factor_block(work[pl.ds(at, BLK), pl.ds(at, BLK)])
        diag[kb] = upper
        strip = jnp.dot(inverse, work[pl.ds(at, BLK), :], precision=HI, preferred_element_type=F32)
        work[pl.ds(at, BLK), :] = strip
        work[pl.ds(at, BLK), pl.ds(at, BLK)] = inverse

        @pl.loop(kb + 1, blocks)
        def _(rb):
            to = pl.multiple_of(rb * BLK, BLK)
            change = dot_tn(work[pl.ds(at, BLK), pl.ds(to, BLK)], work[pl.ds(at, BLK), :])
            old = work[pl.ds(to, BLK), :]
            work[pl.ds(to, BLK), :] = jnp.where(lane_blk == kb, F32(0.0), old) - change

    for r in range(blocks):
        winv[r * BLK:(r + 1) * BLK, :] = jnp.where(
            lane_blk <= r, work[r * BLK:(r + 1) * BLK, :], F32(0.0))
    lower[...] = jnp.zeros_like(lower)
    for r in range(blocks):
        for s in range(r + 1):
            which = (r // 4) + (s // 4)
            src = diag[r] if r == s else work[s * BLK:(s + 1) * BLK, r * BLK:(r + 1) * BLK]
            lower[which, (r % 4) * BLK:(r % 4 + 1) * BLK, (s % 4) * BLK:(s % 4 + 1) * BLK] = src.T


def factorize(head):
    return pl.pallas_call(
        factor_kernel,
        out_shape=(
            jax.ShapeDtypeStruct((3, 512, 512), F32),
            jax.ShapeDtypeStruct((1024, 1024), F32),
        ),
        scratch_shapes=[pltpu.VMEM((1024, 1024), F32), pltpu.VMEM((8, BLK, BLK), F32)],
        compiler_params=pltpu.CompilerParams(vmem_limit_bytes=40 * 1024 * 1024),
        name="factorize",
    )(head)


def halves(x):
    high = x.astype(BF16)
    return high, (x - high.astype(F32)).astype(BF16)


def dot_nt3(lhs, rhs):
    def one(p, q):
        return lax.dot_general(p, q, (((1,), (1,)), ((), ())), preferred_element_type=F32)
    return one(lhs[0], rhs[0]) + (one(lhs[0], rhs[1]) + one(lhs[1], rhs[0]))


def solve_kernel(panel, winv, high, low, whigh, wlow):
    @pl.when(pl.program_id(0) == 0)
    def _():
        top, rest = halves(winv[...])
        whigh[...] = top
        wlow[...] = rest

    top, rest = halves(panel[0])
    first = dot_nt3((top[:, :512], rest[:, :512]), (whigh[:512, :512], wlow[:512, :512]))
    second = dot_nt3((top, rest), (whigh[512:, :], wlow[512:, :]))
    high[0, :, :512], low[0, :, :512] = halves(first)
    high[0, :, 512:], low[0, :, 512:] = halves(second)


def solve_panels(panels, winv):
    block = pl.BlockSpec((1, 512, 1024), lambda i: (i, 0, 0))
    return pl.pallas_call(
        solve_kernel,
        grid=(6,),
        out_shape=(jax.ShapeDtypeStruct((6, 512, 1024), BF16),) * 2,
        in_specs=[block, pl.BlockSpec((1024, 1024), lambda i: (0, 0))],
        out_specs=(block, block),
        scratch_shapes=[pltpu.VMEM((1024, 1024), BF16)] * 2,
        compiler_params=pltpu.CompilerParams(vmem_limit_bytes=40 * 1024 * 1024),
        name="solve",
    )(panels, winv)


def update_kernel(tiles, high_row, low_row, high_col, low_col, lower, out):
    g = lax.axis_index("row")
    c = lax.axis_index("col")
    a, half = pl.program_id(0), pl.program_id(1)
    flat = out.at[0].reshape(512 * 8, 128)
    left = (high_row[0], low_row[0])

    def put(slot, value):
        for n in range(4):
            flat[pl.ds(slot * 4 + n, 512, stride=8), :] = value[:, n * 128:(n + 1) * 128]

    for b in range(2):
        put(b, tiles[0, b] - dot_nt3(left, (high_col[b], low_col[b])))

    @pl.when((half == 0) & (c == 0))
    def _():
        put(0, high_row[0, :, :512].astype(F32) + low_row[0, :, :512].astype(F32))

    @pl.when((half == 0) & (c == 1))
    def _():
        put(0, high_row[0, :, 512:].astype(F32) + low_row[0, :, 512:].astype(F32))

    @pl.when((a == 0) & (g < 2))
    def _():
        flat[...] = jnp.zeros((512 * 8, 128), F32)

        @pl.when((half == 0) & (c <= g))
        def _():
            put(0, lower[g + c])


def update_tiles(tiles, high, low, lower):
    row_block = pl.BlockSpec((1, 512, 1024), lambda a, h: (a, 0, 0))
    col_block = pl.BlockSpec((2, 512, 1024), lambda a, h: (1 + h, 0, 0))
    return pl.pallas_call(
        update_kernel,
        grid=(2, 2),
        out_shape=jax.ShapeDtypeStruct((2, 512, 16, 128), F32),
        in_specs=[
            pl.BlockSpec((1, 2, 512, 512), lambda a, h: (a, h, 0, 0)),
            row_block, row_block, col_block, col_block,
            pl.BlockSpec((3, 512, 512), lambda a, h: (0, 0, 0)),
        ],
        out_specs=pl.BlockSpec((1, 512, 8, 128), lambda a, h: (a, 0, h, 0)),
        compiler_params=pltpu.CompilerParams(vmem_limit_bytes=56 * 1024 * 1024),
        name="update",
    )(tiles, high, low, high, low, lower)


def shards(kernel_rows):
    rows = kernel_rows.reshape(2, 64, 16384)
    tiles, panels, head = exchange(rows)
    lower, winv = factorize(head)
    high, low = solve_panels(panels, winv)
    out = update_tiles(tiles, high, low, lower)
    return out.reshape(2, 1, 512, 4, 1, 512)


def solution(mesh):
    return jax.shard_map(
        shards,
        mesh=mesh,
        in_specs=(P(None, "row", "col", None, None),),
        out_specs=P(None, "row", None, None, "col", None),
        check_vma=False,
    )
```

```python
import functools
import jax
import jax.numpy as jnp
from jax import lax
from jax.experimental import pallas as pl
from jax.experimental.pallas import tpu as pltpu
from jax.sharding import PartitionSpec as P

MESH = pl.DeviceIdType.MESH
HI = lax.Precision.HIGHEST
F32 = jnp.float32
BF16 = jnp.bfloat16
BLK = 128
STRIP = 8
VMEM_CAP = 64 * 1024 * 1024 - 128 * 1024


def dot_tn(lhs, rhs):
    return lax.dot_general(lhs, rhs, (((0,), (0,)), ((), ())), precision=HI,
                           preferred_element_type=F32)


def factor_block(block):
    count = BLK // STRIP
    lane = lax.broadcasted_iota(jnp.int32, (STRIP, BLK), 1)
    sublane = lax.broadcasted_iota(jnp.int32, (STRIP, BLK), 0)
    left = [block[STRIP * t:STRIP * (t + 1), :] for t in range(count)]
    right = [jnp.where(lane == sublane + STRIP * t, F32(1.0), F32(0.0)) for t in range(count)]
    upper, inverse = [], []
    for t in range(count):
        row = [jnp.broadcast_to(left[t][i:i + 1, :], (STRIP, BLK)) for i in range(STRIP)]
        inv = [jnp.broadcast_to(right[t][i:i + 1, :], (STRIP, BLK)) for i in range(STRIP)]
        entry = {}
        for i in range(STRIP):
            for j in range(i, STRIP):
                at = STRIP * t + j
                entry[i, j] = jnp.broadcast_to(row[i][:, at:at + 1], (STRIP, BLK))
        for k in range(STRIP):
            scale = lax.rsqrt(entry[k, k])
            row[k] = row[k] * scale
            inv[k] = inv[k] * scale
            factor = {i: entry[k, i] * scale for i in range(k + 1, STRIP)}
            for i in range(k + 1, STRIP):
                for j in range(i, STRIP):
                    entry[i, j] = entry[i, j] - factor[i] * factor[j]
                row[i] = row[i] - factor[i] * row[k]
                inv[i] = inv[i] - factor[i] * inv[k]
        strip_row, strip_inv = row[0], inv[0]
        for i in range(1, STRIP):
            strip_row = jnp.where(sublane == i, row[i], strip_row)
            strip_inv = jnp.where(sublane == i, inv[i], strip_inv)
        strip_row = jnp.where(lane >= sublane + STRIP * t, strip_row, F32(0.0))
        upper.append(strip_row)
        inverse.append(strip_inv)
        if t + 1 < count:
            change = dot_tn(strip_row, jnp.concatenate([strip_row, strip_inv], axis=1))
            for s in range(t + 1, count):
                left[s] = left[s] - change[STRIP * s:STRIP * (s + 1), :BLK]
                right[s] = right[s] - change[STRIP * s:STRIP * (s + 1), BLK:]
    return jnp.concatenate(upper, axis=0), jnp.concatenate(inverse, axis=0)


def halves(x):
    high = x.astype(BF16)
    return high, (x - high.astype(F32)).astype(BF16)


def dot_nt3(lhs, rhs):
    def one(p, q):
        return lax.dot_general(p, q, (((1,), (1,)), ((), ())), preferred_element_type=F32)
    return one(lhs[0], rhs[0]) + (one(lhs[0], rhs[1]) + one(lhs[1], rhs[0]))


def dot_nn3(lhs, rhs):
    def one(p, q):
        return jnp.dot(p, q, preferred_element_type=F32)
    return one(lhs[0], rhs[0]) + (one(lhs[0], rhs[1]) + one(lhs[1], rhs[0]))


(SPREAD0, SPREAD1, SPREAD2, HEAD_A, HEAD_B, ACROSS_A, ACROSS_B, PAIR_A, PAIR_B, ROWS, ROWS_PAIR,
 ROWS_ON, SWAP, FIRST_Z, FIRST_Y, THEN_Y, THEN_Z, TILES) = range(18)
L_SLAB, L_OWN, L_HEAD, L_ROWS, L_SWAP, L_TILES, L_IN, L_OUT = 0, 1, 2, 3, 4, 5, 6, 8


def exchange_kernel(kr, tiles, panels, high, low, lower, slab, own, head, work, diag, whigh, wlow,
                    inbuf, hbuf, lbuf, ssem, rsem, lsem):
    g = lax.axis_index("row")
    c = lax.axis_index("col")
    core = lax.rem(c, 2)
    other = (c // 2) * 2 + 1 - core
    y, z = g // 4, lax.rem(g, 4)
    swap_row = (g // 8) * 8 + c
    swap_col = lax.rem(g, 8)
    is_self = swap_col == c
    mine = pl.multiple_of(c * 64, 64)
    not_self = jnp.logical_not(is_self)

    def send(src, dst, index, row, col):
        pltpu.make_async_remote_copy(
            src_ref=src, dst_ref=dst, send_sem=ssem.at[index], recv_sem=rsem.at[index],
            device_id=(row, col), device_id_type=MESH).start()

    def local(src, dst, index):
        pltpu.make_async_copy(src, dst, lsem.at[index]).start()

    def done(ref, sem):
        pltpu.make_async_copy(ref, ref, sem).wait()

    local(kr.at[:, :, pl.ds(0, 1024)], slab, L_SLAB)
    for a in range(2):
        for b in range(4):
            at = pl.multiple_of((b * 8 + c) * 512, 512)
            local(kr.at[a, :, pl.ds(at, 512)], own.at[a, b], L_OWN)

    barrier = pltpu.get_barrier_semaphore()

    @pl.loop(1, 16)
    def _(o):
        pl.semaphore_signal(barrier, inc=1, device_id=(lax.rem(g + o, 16), c), device_id_type=MESH)

    @pl.loop(1, 8)
    def _(o):
        pl.semaphore_signal(barrier, inc=1, device_id=(g, lax.rem(c + o, 8)), device_id_type=MESH)

    @pl.when(not_self)
    def _():
        pl.semaphore_signal(barrier, inc=1, device_id=(swap_row, swap_col), device_id_type=MESH)
        pl.semaphore_wait(barrier, 23)

    @pl.when(is_self)
    def _():
        pl.semaphore_wait(barrier, 22)

    done(slab, lsem.at[L_SLAB])

    def piece(which, q):
        return head.at[which, pl.ds(pl.multiple_of(mine + (q // 2) * 8, 8), 8),
                       pl.ds(pl.multiple_of(lax.rem(q, 2) * 256, 256), 256)]

    def spread(which, root, lanes_at, index):
        def src(q):
            return slab.at[0, pl.ds(pl.multiple_of((q // 2) * 8, 8), 8),
                           pl.ds(pl.multiple_of(lanes_at + lax.rem(q, 2) * 256, 256), 256)]

        @pl.when(g == root)
        def _():
            @pl.loop(1, 16)
            def _(o):
                q = lax.rem(g + o, 16)
                send(src(q), piece(which, q), index, q, c)
            local(src(g), piece(which, g), L_HEAD)

    spread(0, 0, 0, SPREAD0)
    spread(2, 1, 512, SPREAD2)
    spread(1, 0, 512, SPREAD1)

    def col_slab(a, r):
        return panels.at[2 + r // 8 + 2 * a, pl.ds(pl.multiple_of(lax.rem(r, 8) * 64, 64), 64), :]

    @pl.when(not_self)
    def _():
        for a in range(2):
            send(slab.at[a], col_slab(a, swap_row), SWAP, swap_row, swap_col)

    @pl.when(is_self)
    def _():
        for a in range(2):
            local(slab.at[a], col_slab(a, g), L_SWAP)

    def send_tiles(first, last):
        @pl.loop(1, 8)
        def _(o):
            cc = lax.rem(c + o, 8)
            for n in range(first, last):
                a, b = n // 4, n % 4
                at = pl.multiple_of((b * 8 + cc) * 512, 512)
                send(kr.at[a, :, pl.ds(at, 512)], tiles.at[a, b, pl.ds(mine, 64), :], TILES, g, cc)

    send_tiles(0, 1)

    def gather_head(which, index):
        @pl.loop(1, 16)
        def _(o):
            send(piece(which, g), piece(which, g), index, lax.rem(g + o, 16), c)

    def chunk(which, col):
        return head.at[which, pl.ds(pl.multiple_of(col * 64, 64), 64), :]

    def across(which, index):
        for o in range(1, 4):
            send(chunk(which, c), chunk(which, c), index, g, lax.rem(c + 2 * o, 8))

    def pair(which, index):
        for o in range(4):
            src = chunk(which, lax.rem(c + 2 * o, 8))
            send(src, src, index, g, other)

    @pl.when(g == 0)
    def _():
        done(head.at[0, pl.ds(0, 16), pl.ds(0, 256)], lsem.at[L_HEAD])

    @pl.when(g == 1)
    def _():
        done(head.at[0, pl.ds(0, 8), pl.ds(0, 256)], lsem.at[L_HEAD])

    @pl.when(g != 0)
    def _():
        done(piece(0, g), rsem.at[SPREAD0])

    gather_head(0, HEAD_A)

    @pl.when(g != 0)
    def _():
        done(piece(1, g), rsem.at[SPREAD1])

    @pl.when(g != 1)
    def _():
        done(piece(2, g), rsem.at[SPREAD2])

    gather_head(1, HEAD_B)
    gather_head(2, HEAD_B)
    done(head.at[0, pl.ds(0, 120), pl.ds(0, 256)], rsem.at[HEAD_A])
    across(0, ACROSS_A)
    done(head.at[1, pl.ds(0, 240), pl.ds(0, 256)], rsem.at[HEAD_B])
    across(1, ACROSS_B)
    across(2, ACROSS_B)

    for a in range(2):
        dst = panels.at[a, pl.ds(mine, 64), :]
        for o in range(1, 4):
            send(slab.at[a], dst, ROWS, g, lax.rem(c + 2 * o, 8))
        send(slab.at[a], dst, ROWS_PAIR, g, other)
        local(slab.at[a], dst, L_ROWS)

    send_tiles(1, 8)
    done(own, lsem.at[L_OWN])
    for a in range(2):
        for b in range(4):
            local(own.at[a, b], tiles.at[a, b, pl.ds(mine, 64), :], L_TILES)

    done(head.at[0, pl.ds(0, 192), :], rsem.at[ACROSS_A])
    pair(0, PAIR_A)

    @pl.when(not_self)
    def _():
        done(slab, rsem.at[SWAP])

    @pl.when(is_self)
    def _():
        done(slab, lsem.at[L_SWAP])

    def row_of(dy, dz):
        return lax.rem(y + dy, 4) * 4 + lax.rem(z + dz, 4)

    for o in range(1, 4):
        send(col_slab(0, g), col_slab(0, g), FIRST_Z, row_of(0, o), c)
        send(col_slab(1, g), col_slab(1, g), FIRST_Y, row_of(o, 0), c)

    def second_stage():
        three = panels.at[0, pl.ds(0, 192), :]
        done(three, rsem.at[FIRST_Z])
        done(three, rsem.at[FIRST_Y])

        @pl.loop(0, 4)
        def _(n):
            from_z, from_y = row_of(0, n), row_of(n, 0)
            for o in range(1, 4):
                send(col_slab(0, from_z), col_slab(0, from_z), THEN_Y, row_of(o, 0), c)
                send(col_slab(1, from_y), col_slab(1, from_y), THEN_Z, row_of(0, o), c)

    def rows_on():
        done(panels.at[0, pl.ds(0, 384), :], rsem.at[ROWS])
        for a in range(2):
            for o in range(1, 4):
                at = pl.multiple_of(lax.rem(c + 2 * o, 8) * 64, 64)
                src = panels.at[a, pl.ds(at, 64), :]
                send(src, src, ROWS_ON, g, other)

    done(head.at[0, pl.ds(0, 256), :], rsem.at[PAIR_A])

    lane_blk = lax.broadcasted_iota(jnp.int32, (BLK, 512), 1) // BLK
    blocks = 512 // BLK

    def factor(panel, between):
        @pl.loop(0, blocks)
        def _(kb):
            at = pl.multiple_of(kb * BLK, BLK)
            upper, inverse = factor_block(work[pl.ds(at, BLK), pl.ds(at, BLK)])
            diag[panel * blocks + kb] = upper
            strip = jnp.dot(inverse, work[pl.ds(at, BLK), :], precision=HI,
                            preferred_element_type=F32)
            work[pl.ds(at, BLK), :] = strip
            work[pl.ds(at, BLK), pl.ds(at, BLK)] = inverse

            @pl.loop(kb + 1, blocks)
            def _(rb):
                to = pl.multiple_of(rb * BLK, BLK)
                change = dot_tn(work[pl.ds(at, BLK), pl.ds(to, BLK)], work[pl.ds(at, BLK), :])
                old = work[pl.ds(to, BLK), :]
                work[pl.ds(to, BLK), :] = jnp.where(lane_blk == kb, F32(0.0), old) - change

            between(kb)

        for r in range(blocks):
            here = slice(r * BLK, (r + 1) * BLK)
            row = jnp.where(lane_blk <= r, work[here, :], F32(0.0))
            whigh[2 * panel, here, :], wlow[2 * panel, here, :] = halves(row)
            for s in range(blocks):
                there = slice(s * BLK, (s + 1) * BLK)
                if s > r:
                    lower[2 * panel, here, there] = jnp.zeros((BLK, BLK), F32)
                elif s == r:
                    lower[2 * panel, here, there] = diag[panel * blocks + r].T
                else:
                    lower[2 * panel, here, there] = work[there, here].T

    work[...] = head[0]

    def between(kb):
        @pl.when(kb == 0)
        def _():
            done(head.at[1, pl.ds(0, 384), :], rsem.at[ACROSS_B])
            pair(1, PAIR_B)
            pair(2, PAIR_B)

        @pl.when(kb == 1)
        def _():
            second_stage()

        @pl.when(kb == 3)
        def _():
            rows_on()

    factor(0, between)
    done(head.at[pl.ds(1, 2), pl.ds(0, 256), :], rsem.at[PAIR_B])

    right = dot_nn3((whigh[0], wlow[0]), halves(head[1]))
    whigh[1], wlow[1] = halves(right)
    lower[1] = right.T
    work[...] = head[2] - dot_tn(right, right)
    factor(1, lambda kb: None)

    done(panels.at[0, pl.ds(0, 128), :], rsem.at[ROWS_PAIR])
    done(panels.at[0, pl.ds(0, 384), :], rsem.at[ROWS_ON])
    done(slab, lsem.at[L_ROWS])
    twelve = panels.at[pl.ds(0, 2), pl.ds(0, 384), :]
    done(twelve, rsem.at[THEN_Y])
    done(twelve, rsem.at[THEN_Z])

    def fetch(t, slot):
        return pltpu.make_async_copy(panels.at[t], inbuf.at[slot], lsem.at[L_IN + slot])

    def store(t, slot):
        return (pltpu.make_async_copy(hbuf.at[slot], high.at[t], lsem.at[L_OUT + slot]),
                pltpu.make_async_copy(lbuf.at[slot], low.at[t], lsem.at[L_OUT + 2 + slot]))

    fetch(0, 0).start()

    @pl.loop(0, 6)
    def _(t):
        slot = lax.rem(t, 2)

        @pl.when(t < 5)
        def _():
            fetch(t + 1, 1 - slot).start()

        fetch(t, slot).wait()

        @pl.when(t >= 2)
        def _():
            for cp in store(t - 2, slot):
                cp.wait()

        first = dot_nt3(halves(inbuf[slot, :, :512]), (whigh[0], wlow[0]))
        top, rest = halves(first)
        hbuf[slot, :, :512], lbuf[slot, :, :512] = top, rest
        left = inbuf[slot, :, 512:] - dot_nn3((top, rest), (whigh[1], wlow[1]))
        hbuf[slot, :, 512:], lbuf[slot, :, 512:] = halves(
            dot_nt3(halves(left), (whigh[2], wlow[2])))
        for cp in store(t, slot):
            cp.start()

    for t in range(4, 6):
        for cp in store(t, t % 2):
            cp.wait()

    done(own, lsem.at[L_TILES])
    done(tiles.at[:, :, pl.ds(0, 448), :], rsem.at[TILES])
    done(tiles.at[:, :, pl.ds(0, 448), :], ssem.at[TILES])

    @pl.when(g == 0)
    def _():
        done(head.at[0, pl.ds(0, 120), pl.ds(0, 256)], ssem.at[SPREAD0])
        done(head.at[0, pl.ds(0, 120), pl.ds(0, 256)], ssem.at[SPREAD1])

    @pl.when(g == 1)
    def _():
        done(head.at[0, pl.ds(0, 120), pl.ds(0, 256)], ssem.at[SPREAD2])

    done(head.at[0, pl.ds(0, 120), pl.ds(0, 256)], ssem.at[HEAD_A])
    done(head.at[1, pl.ds(0, 240), pl.ds(0, 256)], ssem.at[HEAD_B])
    done(head.at[0, pl.ds(0, 192), :], ssem.at[ACROSS_A])
    done(head.at[1, pl.ds(0, 384), :], ssem.at[ACROSS_B])
    done(head.at[0, pl.ds(0, 256), :], ssem.at[PAIR_A])
    done(head.at[pl.ds(1, 2), pl.ds(0, 256), :], ssem.at[PAIR_B])
    done(panels.at[0, pl.ds(0, 384), :], ssem.at[ROWS])
    done(panels.at[0, pl.ds(0, 128), :], ssem.at[ROWS_PAIR])
    done(panels.at[0, pl.ds(0, 384), :], ssem.at[ROWS_ON])

    @pl.when(not_self)
    def _():
        done(slab, ssem.at[SWAP])

    three = panels.at[0, pl.ds(0, 192), :]
    done(three, ssem.at[FIRST_Z])
    done(three, ssem.at[FIRST_Y])
    done(twelve, ssem.at[THEN_Y])
    done(twelve, ssem.at[THEN_Z])


def exchange(rows):
    anyspace = pl.BlockSpec(memory_space=pl.ANY)
    return pl.pallas_call(
        exchange_kernel,
        out_shape=(
            jax.ShapeDtypeStruct((2, 4, 512, 512), F32),
            jax.ShapeDtypeStruct((6, 512, 1024), F32),
            jax.ShapeDtypeStruct((6, 512, 1024), BF16),
            jax.ShapeDtypeStruct((6, 512, 1024), BF16),
            jax.ShapeDtypeStruct((3, 512, 512), F32),
        ),
        in_specs=[anyspace],
        out_specs=(anyspace,) * 4 + (pl.BlockSpec(memory_space=pltpu.VMEM),),
        scratch_shapes=[
            pltpu.VMEM((2, 64, 1024), F32),
            pltpu.VMEM((2, 4, 64, 512), F32),
            pltpu.VMEM((3, 512, 512), F32),
            pltpu.VMEM((512, 512), F32),
            pltpu.VMEM((8, BLK, BLK), F32),
            pltpu.VMEM((3, 512, 512), BF16),
            pltpu.VMEM((3, 512, 512), BF16),
            pltpu.VMEM((2, 512, 1024), F32),
            pltpu.VMEM((2, 512, 1024), BF16),
            pltpu.VMEM((2, 512, 1024), BF16),
            pltpu.SemaphoreType.DMA((18,)),
            pltpu.SemaphoreType.DMA((18,)),
            pltpu.SemaphoreType.DMA((12,)),
        ],
        compiler_params=pltpu.CompilerParams(
            collective_id=1, has_side_effects=True, vmem_limit_bytes=48 * 1024 * 1024),
        name="exchange",
    )(rows)


def update_kernel(tiles, high_row, low_row, high_col, low_col, lower, out):
    g = lax.axis_index("row")
    c = lax.axis_index("col")
    a, half = pl.program_id(0), pl.program_id(1)
    flat = out.at[0].reshape(512 * 8, 128)
    left = (high_row[0], low_row[0])

    def put(slot, value):
        for n in range(4):
            flat[pl.ds(slot * 4 + n, 512, stride=8), :] = value[:, n * 128:(n + 1) * 128]

    for b in range(2):
        put(b, tiles[0, b] - dot_nt3(left, (high_col[b], low_col[b])))

    @pl.when((half == 0) & (c == 0))
    def _():
        put(0, high_row[0, :, :512].astype(F32) + low_row[0, :, :512].astype(F32))

    @pl.when((half == 0) & (c == 1))
    def _():
        put(0, high_row[0, :, 512:].astype(F32) + low_row[0, :, 512:].astype(F32))

    @pl.when((a == 0) & (g < 2))
    def _():
        flat[...] = jnp.zeros((512 * 8, 128), F32)

        @pl.when((half == 0) & (c <= g))
        def _():
            put(0, lower[g + c])


def update_tiles(tiles, high, low, lower):
    row_block = pl.BlockSpec((1, 512, 1024), lambda a, h: (a, 0, 0))
    col_block = pl.BlockSpec((2, 512, 1024), lambda a, h: (1 + h, 0, 0))
    return pl.pallas_call(
        update_kernel,
        grid=(2, 2),
        out_shape=jax.ShapeDtypeStruct((2, 512, 16, 128), F32),
        in_specs=[
            pl.BlockSpec((1, 2, 512, 512), lambda a, h: (a, h, 0, 0)),
            row_block, row_block, col_block, col_block,
            pl.BlockSpec((3, 512, 512), lambda a, h: (0, 0, 0)),
        ],
        out_specs=pl.BlockSpec((1, 512, 8, 128), lambda a, h: (a, 0, h, 0)),
        compiler_params=pltpu.CompilerParams(vmem_limit_bytes=56 * 1024 * 1024),
        name="update",
    )(tiles, high, low, high, low, lower)


def shards(kernel_rows):
    rows = kernel_rows.reshape(2, 64, 16384)
    tiles, panels, high, low, lower = exchange(rows)
    out = update_tiles(tiles, high, low, lower)
    return out.reshape(2, 1, 512, 4, 1, 512)


def solution(mesh):
    return jax.shard_map(
        shards,
        mesh=mesh,
        in_specs=(P(None, "row", "col", None, None),),
        out_specs=P(None, "row", None, None, "col", None),
        check_vma=False,
    )
```

```python
import functools
import jax
import jax.numpy as jnp
from jax import lax
from jax.experimental import pallas as pl
from jax.experimental.pallas import tpu as pltpu
from jax.sharding import PartitionSpec as P

MESH = pl.DeviceIdType.MESH
HI = lax.Precision.HIGHEST
F32 = jnp.float32
BF16 = jnp.bfloat16
BLK = 128
STRIP = 8


def dot_tn(lhs, rhs):
    return lax.dot_general(lhs, rhs, (((0,), (0,)), ((), ())), precision=HI,
                           preferred_element_type=F32)


def factor_block(block):
    count = BLK // STRIP
    lane = lax.broadcasted_iota(jnp.int32, (STRIP, BLK), 1)
    sublane = lax.broadcasted_iota(jnp.int32, (STRIP, BLK), 0)
    zero, one = F32(0.0), F32(1.0)
    span = range(STRIP)
    strips = [block[STRIP * t:STRIP * (t + 1), :] for t in range(count)]
    solved = []

    def whole(strip, i):
        return jnp.broadcast_to(strip[i:i + 1, :], (STRIP, BLK))

    def single(strip, at):
        return jnp.broadcast_to(strip[:, at:at + 1], (STRIP, BLK))

    here_strip = strips[0]
    cols = [single(here_strip, j) for j in span]
    for t in range(count):
        more = t + 1 < count
        here = (lane >= STRIP * t) & (lane < STRIP * (t + 1))
        here_strip = jnp.where(here, jnp.where(lane == STRIP * t + sublane, one, zero), here_strip)
        if more:
            pick = lane == STRIP * (t + 1) + sublane
            next_strip = jnp.where(here, zero, strips[t + 1])
            next_cols = [single(next_strip, STRIP * (t + 1) + j) for j in span]
            sum_strip, sum_cols = None, [None] * STRIP
        for k in span:
            scale = lax.rsqrt(whole(cols[k], k))
            factor = cols[k] * scale
            for j in range(k + 1, STRIP):
                cols[j] = cols[j] - factor * whole(factor, j)
            row = whole(here_strip, k) * scale
            below = jnp.where(sublane > k, factor, zero)
            here_strip = jnp.where(sublane == k, row, here_strip - below * row)
            if more:
                across = jnp.sum(jnp.where(pick, row, zero), axis=1, keepdims=True)
                across = jnp.broadcast_to(across, (STRIP, BLK))
                terms = [across * row] + [across * whole(across, j) for j in span]
                if k == 0:
                    sum_strip, sum_cols = terms[0], terms[1:]
                elif k < STRIP - 1:
                    sum_strip = sum_strip + terms[0]
                    sum_cols = [p + q for p, q in zip(sum_cols, terms[1:])]
                else:
                    next_strip = (next_strip - sum_strip) - terms[0]
                    next_cols = [(b - p) - q for b, p, q in zip(next_cols, sum_cols, terms[1:])]
        solved.append(here_strip)
        if more:
            last_strip = here_strip
            here_strip, cols = next_strip, next_cols
        if t + 2 < count:
            change = dot_tn(last_strip, last_strip)
            for s in range(t + 2, count):
                strips[s] = jnp.where(here, zero, strips[s]) - change[STRIP * s:STRIP * (s + 1), :]
    return jnp.concatenate(
        [jnp.where(lane < STRIP * (t + 1), solved[t], zero) for t in range(count)], axis=0)


def halves(x):
    high = x.astype(BF16)
    return high, (x - high.astype(F32)).astype(BF16)


def dot_nt3(lhs, rhs):
    def one(p, q):
        return lax.dot_general(p, q, (((1,), (1,)), ((), ())), preferred_element_type=F32)
    return one(lhs[0], rhs[0]) + (one(lhs[0], rhs[1]) + one(lhs[1], rhs[0]))


def dot_nn3(lhs, rhs):
    def one(p, q):
        return jnp.dot(p, q, preferred_element_type=F32)
    return one(lhs[0], rhs[0]) + (one(lhs[0], rhs[1]) + one(lhs[1], rhs[0]))


(SPREAD0, SPREAD1, SPREAD2, HEAD_A, HEAD_B, ACROSS_A, ACROSS_B, PAIR_A, PAIR_B, ROWS, ROWS_PAIR,
 ROWS_ON, SWAP, FIRST_Z, FIRST_Y, THEN_Y, THEN_Z, TILES) = range(18)
SEMS = TILES + 8
L_SLAB, L_OWN, L_HEAD, L_ROWS, L_SWAP, L_IN, L_OUT = 0, 1, 2, 3, 4, 5, 7


def exchange_kernel(kr, out, panels, tiles, slab, head, work, diag, lower, whigh, wlow,
                    inbuf, high, low, obuf, ssem, rsem, lsem):
    g = lax.axis_index("row")
    c = lax.axis_index("col")
    core = lax.rem(c, 2)
    other = (c // 2) * 2 + 1 - core
    y, z = g // 4, lax.rem(g, 4)
    swap_row = (g // 8) * 8 + c
    swap_col = lax.rem(g, 8)
    is_self = swap_col == c
    mine = pl.multiple_of(c * 64, 64)
    not_self = jnp.logical_not(is_self)

    def send(src, dst, index, row, col):
        pltpu.make_async_remote_copy(
            src_ref=src, dst_ref=dst, send_sem=ssem.at[index], recv_sem=rsem.at[index],
            device_id=(row, col), device_id_type=MESH).start()

    def local(src, dst, index):
        pltpu.make_async_copy(src, dst, lsem.at[index]).start()

    def done(ref, sem):
        pltpu.make_async_copy(ref, ref, sem).wait()

    local(kr.at[:, :, pl.ds(0, 1024)], slab, L_SLAB)
    for a in range(2):
        for b in range(4):
            at = pl.multiple_of((b * 8 + c) * 512, 512)
            local(kr.at[a, :, pl.ds(at, 512)], tiles.at[a * 4 + b, pl.ds(mine, 64), :], L_OWN)

    barrier = pltpu.get_barrier_semaphore()

    @pl.loop(1, 16)
    def _(o):
        pl.semaphore_signal(barrier, inc=1, device_id=(lax.rem(g + o, 16), c), device_id_type=MESH)

    @pl.loop(1, 8)
    def _(o):
        pl.semaphore_signal(barrier, inc=1, device_id=(g, lax.rem(c + o, 8)), device_id_type=MESH)

    @pl.when(not_self)
    def _():
        pl.semaphore_signal(barrier, inc=1, device_id=(swap_row, swap_col), device_id_type=MESH)
        pl.semaphore_wait(barrier, 23)

    @pl.when(is_self)
    def _():
        pl.semaphore_wait(barrier, 22)

    done(slab, lsem.at[L_SLAB])

    def piece(which, q):
        return head.at[which, pl.ds(pl.multiple_of(mine + (q // 2) * 8, 8), 8),
                       pl.ds(pl.multiple_of(lax.rem(q, 2) * 256, 256), 256)]

    def spread(which, root, lanes_at, index):
        def src(q):
            return slab.at[0, pl.ds(pl.multiple_of((q // 2) * 8, 8), 8),
                           pl.ds(pl.multiple_of(lanes_at + lax.rem(q, 2) * 256, 256), 256)]

        @pl.when(g == root)
        def _():
            @pl.loop(1, 16)
            def _(o):
                q = lax.rem(g + o, 16)
                send(src(q), piece(which, q), index, q, c)
            local(src(g), piece(which, g), L_HEAD)

    spread(0, 0, 0, SPREAD0)
    spread(2, 1, 512, SPREAD2)
    spread(1, 0, 512, SPREAD1)

    def col_slab(a, r):
        return panels.at[2 + r // 8 + 2 * a, pl.ds(pl.multiple_of(lax.rem(r, 8) * 64, 64), 64), :]

    @pl.when(not_self)
    def _():
        for a in range(2):
            send(slab.at[a], col_slab(a, swap_row), SWAP, swap_row, swap_col)

    @pl.when(is_self)
    def _():
        for a in range(2):
            local(slab.at[a], col_slab(a, g), L_SWAP)

    def send_tiles():
        @pl.loop(0, 8)
        def _(n):
            @pl.loop(1, 8)
            def _(o):
                cc = lax.rem(c + o, 8)
                at = pl.multiple_of((lax.rem(n, 4) * 8 + cc) * 512, 512)
                send(kr.at[n // 4, :, pl.ds(at, 512)], tiles.at[n, pl.ds(mine, 64), :],
                     TILES + n, g, cc)

    def gather_head(which, index):
        @pl.loop(1, 16)
        def _(o):
            send(piece(which, g), piece(which, g), index, lax.rem(g + o, 16), c)

    def chunk(which, col):
        return head.at[which, pl.ds(pl.multiple_of(col * 64, 64), 64), :]

    def across(which, index):
        for o in range(1, 4):
            send(chunk(which, c), chunk(which, c), index, g, lax.rem(c + 2 * o, 8))

    def pair(which, index):
        for o in range(4):
            src = chunk(which, lax.rem(c + 2 * o, 8))
            send(src, src, index, g, other)

    @pl.when(g == 0)
    def _():
        done(head.at[0, pl.ds(0, 16), pl.ds(0, 256)], lsem.at[L_HEAD])

    @pl.when(g == 1)
    def _():
        done(head.at[0, pl.ds(0, 8), pl.ds(0, 256)], lsem.at[L_HEAD])

    @pl.when(g != 0)
    def _():
        done(piece(0, g), rsem.at[SPREAD0])

    gather_head(0, HEAD_A)

    @pl.when(g != 0)
    def _():
        done(piece(1, g), rsem.at[SPREAD1])

    @pl.when(g != 1)
    def _():
        done(piece(2, g), rsem.at[SPREAD2])

    gather_head(1, HEAD_B)
    gather_head(2, HEAD_B)
    done(head.at[0, pl.ds(0, 120), pl.ds(0, 256)], rsem.at[HEAD_A])
    across(0, ACROSS_A)
    done(head.at[1, pl.ds(0, 240), pl.ds(0, 256)], rsem.at[HEAD_B])
    across(1, ACROSS_B)
    across(2, ACROSS_B)

    for a in range(2):
        dst = panels.at[a, pl.ds(mine, 64), :]
        for o in range(1, 4):
            send(slab.at[a], dst, ROWS, g, lax.rem(c + 2 * o, 8))
        send(slab.at[a], dst, ROWS_PAIR, g, other)
        local(slab.at[a], dst, L_ROWS)

    send_tiles()
    done(head.at[0, pl.ds(0, 192), :], rsem.at[ACROSS_A])
    pair(0, PAIR_A)

    @pl.when(not_self)
    def _():
        done(slab, rsem.at[SWAP])

    @pl.when(is_self)
    def _():
        done(slab, lsem.at[L_SWAP])

    def row_of(dy, dz):
        return lax.rem(y + dy, 4) * 4 + lax.rem(z + dz, 4)

    for o in range(1, 4):
        send(col_slab(0, g), col_slab(0, g), FIRST_Z, row_of(0, o), c)
        send(col_slab(1, g), col_slab(1, g), FIRST_Y, row_of(o, 0), c)

    def second_stage():
        three = panels.at[0, pl.ds(0, 192), :]
        done(three, rsem.at[FIRST_Z])
        done(three, rsem.at[FIRST_Y])

        @pl.loop(0, 4)
        def _(n):
            from_z, from_y = row_of(0, n), row_of(n, 0)
            for o in range(1, 4):
                send(col_slab(0, from_z), col_slab(0, from_z), THEN_Y, row_of(o, 0), c)
                send(col_slab(1, from_y), col_slab(1, from_y), THEN_Z, row_of(0, o), c)

    def rows_on():
        done(panels.at[0, pl.ds(0, 384), :], rsem.at[ROWS])
        for a in range(2):
            for o in range(1, 4):
                at = pl.multiple_of(lax.rem(c + 2 * o, 8) * 64, 64)
                src = panels.at[a, pl.ds(at, 64), :]
                send(src, src, ROWS_ON, g, other)

    done(head.at[0, pl.ds(0, 256), :], rsem.at[PAIR_A])

    lane_blk = lax.broadcasted_iota(jnp.int32, (BLK, 512), 1) // BLK
    blocks = 512 // BLK
    upper = (lax.broadcasted_iota(jnp.int32, (BLK, BLK), 0)
             <= lax.broadcasted_iota(jnp.int32, (BLK, BLK), 1))

    def factor(panel, between):
        @pl.loop(0, blocks)
        def _(kb):
            at = pl.multiple_of(kb * BLK, BLK)
            inverse = factor_block(work[pl.ds(at, BLK), pl.ds(at, BLK)])
            work[pl.ds(at, BLK), :] = jnp.dot(inverse, work[pl.ds(at, BLK), :], precision=HI,
                                              preferred_element_type=F32)
            diag[kb] = jnp.where(upper, work[pl.ds(at, BLK), pl.ds(at, BLK)], F32(0.0))
            work[pl.ds(at, BLK), pl.ds(at, BLK)] = inverse

            @pl.loop(kb + 1, blocks)
            def _(rb):
                to = pl.multiple_of(rb * BLK, BLK)
                change = dot_tn(work[pl.ds(at, BLK), pl.ds(to, BLK)], work[pl.ds(at, BLK), :])
                old = work[pl.ds(to, BLK), :]
                work[pl.ds(to, BLK), :] = jnp.where(lane_blk == kb, F32(0.0), old) - change

            between(kb)

        for r in range(blocks):
            here = slice(r * BLK, (r + 1) * BLK)
            row = jnp.where(lane_blk <= r, work[here, :], F32(0.0))
            whigh[2 * panel, here, :], wlow[2 * panel, here, :] = halves(row)
            for s in range(blocks):
                there = slice(s * BLK, (s + 1) * BLK)
                if s > r:
                    lower[2 * panel, here, there] = jnp.zeros((BLK, BLK), F32)
                elif s == r:
                    lower[2 * panel, here, there] = diag[r].T
                else:
                    lower[2 * panel, here, there] = work[there, here].T

    work[...] = head[0]

    def between(kb):
        @pl.when(kb == 0)
        def _():
            done(head.at[1, pl.ds(0, 384), :], rsem.at[ACROSS_B])
            pair(1, PAIR_B)
            pair(2, PAIR_B)

        @pl.when(kb == 1)
        def _():
            second_stage()

        @pl.when(kb == 3)
        def _():
            rows_on()

    factor(0, between)
    done(head.at[pl.ds(1, 2), pl.ds(0, 256), :], rsem.at[PAIR_B])

    right = dot_nn3((whigh[0], wlow[0]), halves(head[1]))
    whigh[1], wlow[1] = halves(right)
    lower[1] = right.T
    work[...] = head[2] - dot_tn(right, right)
    factor(1, lambda kb: None)

    done(panels.at[0, pl.ds(0, 128), :], rsem.at[ROWS_PAIR])
    done(panels.at[0, pl.ds(0, 384), :], rsem.at[ROWS_ON])
    done(slab, lsem.at[L_ROWS])
    twelve = panels.at[pl.ds(0, 2), pl.ds(0, 384), :]

    def fetch(t, slot):
        return pltpu.make_async_copy(panels.at[t], inbuf.at[slot], lsem.at[L_IN + slot])

    fetch(0, 0).start()

    @pl.loop(0, 6)
    def _(t):
        slot = lax.rem(t, 2)

        @pl.when(t == 1)
        def _():
            done(twelve, rsem.at[THEN_Y])
            done(twelve, rsem.at[THEN_Z])

        @pl.when(t < 5)
        def _():
            fetch(t + 1, 1 - slot).start()

        fetch(t, slot).wait()
        first = dot_nt3(halves(inbuf[slot, :, :512]), (whigh[0], wlow[0]))
        top, rest = halves(first)
        high[t, :, :512], low[t, :, :512] = top, rest
        left = inbuf[slot, :, 512:] - dot_nn3((top, rest), (whigh[1], wlow[1]))
        high[t, :, 512:], low[t, :, 512:] = halves(dot_nt3(halves(left), (whigh[2], wlow[2])))

    done(tiles.at[0], lsem.at[L_OWN])

    def leave(pair_no, slot):
        at = pl.multiple_of(lax.rem(pair_no, 2) * 8, 8)
        return pltpu.make_async_copy(
            obuf.at[slot], out.at[pair_no // 2, :, pl.ds(at, 8), :], lsem.at[L_OUT + slot])

    @pl.loop(0, 8)
    def _(n):
        a, b = n // 4, lax.rem(n, 4)
        pair_no = n // 2
        slot = lax.rem(pair_no, 2)
        half = lax.rem(n, 2)
        flat = obuf.at[slot].reshape(512 * 8, 128)

        def put(value):
            for m in range(4):
                flat[pl.ds(half * 4 + m, 512, stride=8), :] = value[:, m * 128:(m + 1) * 128]

        @pl.when((half == 0) & (pair_no >= 2))
        def _():
            leave(pair_no - 2, slot).wait()

        done(tiles.at[n, pl.ds(0, 448), :], rsem.at[TILES + n])
        special_row = (a == 0) & (g < 2)
        special_col = (b == 0) & (c < 2)

        @pl.when(jnp.logical_not(special_row | special_col))
        def _():
            put(tiles[n] - dot_nt3((high[a], low[a]), (high[2 + b], low[2 + b])))

        @pl.when(special_col & jnp.logical_not(special_row) & (c == 0))
        def _():
            put(high[a, :, :512].astype(F32) + low[a, :, :512].astype(F32))

        @pl.when(special_col & jnp.logical_not(special_row) & (c == 1))
        def _():
            put(high[a, :, 512:].astype(F32) + low[a, :, 512:].astype(F32))

        for corner in range(3):
            @pl.when(special_row & (b == 0) & (c <= g) & (g + c == corner))
            def _():
                put(lower[corner])

        @pl.when(special_row & ((b > 0) | (c > g)))
        def _():
            put(jnp.zeros((512, 512), F32))

        @pl.when(half == 1)
        def _():
            leave(pair_no, slot).start()

    for pair_no in range(2, 4):
        leave(pair_no, pair_no % 2).wait()

    @pl.loop(0, 8)
    def _(n):
        done(tiles.at[n, pl.ds(0, 448), :], ssem.at[TILES + n])

    @pl.when(g == 0)
    def _():
        done(head.at[0, pl.ds(0, 120), pl.ds(0, 256)], ssem.at[SPREAD0])
        done(head.at[0, pl.ds(0, 120), pl.ds(0, 256)], ssem.at[SPREAD1])

    @pl.when(g == 1)
    def _():
        done(head.at[0, pl.ds(0, 120), pl.ds(0, 256)], ssem.at[SPREAD2])

    done(head.at[0, pl.ds(0, 120), pl.ds(0, 256)], ssem.at[HEAD_A])
    done(head.at[1, pl.ds(0, 240), pl.ds(0, 256)], ssem.at[HEAD_B])
    done(head.at[0, pl.ds(0, 192), :], ssem.at[ACROSS_A])
    done(head.at[1, pl.ds(0, 384), :], ssem.at[ACROSS_B])
    done(head.at[0, pl.ds(0, 256), :], ssem.at[PAIR_A])
    done(head.at[pl.ds(1, 2), pl.ds(0, 256), :], ssem.at[PAIR_B])
    done(panels.at[0, pl.ds(0, 384), :], ssem.at[ROWS])
    done(panels.at[0, pl.ds(0, 128), :], ssem.at[ROWS_PAIR])
    done(panels.at[0, pl.ds(0, 384), :], ssem.at[ROWS_ON])

    @pl.when(not_self)
    def _():
        done(slab, ssem.at[SWAP])

    three = panels.at[0, pl.ds(0, 192), :]
    done(three, ssem.at[FIRST_Z])
    done(three, ssem.at[FIRST_Y])
    done(twelve, ssem.at[THEN_Y])
    done(twelve, ssem.at[THEN_Z])


def exchange(rows):
    anyspace = pl.BlockSpec(memory_space=pl.ANY)
    return pl.pallas_call(
        exchange_kernel,
        out_shape=(
            jax.ShapeDtypeStruct((2, 512, 16, 128), F32),
            jax.ShapeDtypeStruct((6, 512, 1024), F32),
        ),
        in_specs=[anyspace],
        out_specs=(anyspace,) * 2,
        scratch_shapes=[
            pltpu.VMEM((8, 512, 512), F32),
            pltpu.VMEM((2, 64, 1024), F32),
            pltpu.VMEM((3, 512, 512), F32),
            pltpu.VMEM((512, 512), F32),
            pltpu.VMEM((4, BLK, BLK), F32),
            pltpu.VMEM((3, 512, 512), F32),
            pltpu.VMEM((3, 512, 512), BF16),
            pltpu.VMEM((3, 512, 512), BF16),
            pltpu.VMEM((2, 512, 1024), F32),
            pltpu.VMEM((6, 512, 1024), BF16),
            pltpu.VMEM((6, 512, 1024), BF16),
            pltpu.VMEM((2, 512, 8, 128), F32),
            pltpu.SemaphoreType.DMA((SEMS,)),
            pltpu.SemaphoreType.DMA((SEMS,)),
            pltpu.SemaphoreType.DMA((9,)),
        ],
        compiler_params=pltpu.CompilerParams(
            collective_id=1, has_side_effects=True, vmem_limit_bytes=56 * 1024 * 1024),
        name="exchange",
    )(rows)


def shards(kernel_rows):
    rows = kernel_rows.reshape(2, 64, 16384)
    out, _ = exchange(rows)
    return out.reshape(2, 1, 512, 4, 1, 512)


def solution(mesh):
    return jax.shard_map(
        shards,
        mesh=mesh,
        in_specs=(P(None, "row", "col", None, None),),
        out_specs=P(None, "row", None, None, "col", None),
        check_vma=False,
    )
```

```python
import functools
import jax
import jax.numpy as jnp
from jax import lax
from jax.experimental import pallas as pl
from jax.experimental.pallas import tpu as pltpu
from jax.sharding import PartitionSpec as P

MESH = pl.DeviceIdType.MESH
HI = lax.Precision.HIGHEST
F32 = jnp.float32
BF16 = jnp.bfloat16
BLK = 128
STRIP = 8


def dot_tn(lhs, rhs):
    return lax.dot_general(lhs, rhs, (((0,), (0,)), ((), ())), precision=HI,
                           preferred_element_type=F32)


def factor_block(block):
    count = BLK // STRIP
    lane = lax.broadcasted_iota(jnp.int32, (STRIP, BLK), 1)
    sublane = lax.broadcasted_iota(jnp.int32, (STRIP, BLK), 0)
    zero, one = F32(0.0), F32(1.0)
    span = range(STRIP)
    strips = [block[STRIP * t:STRIP * (t + 1), :] for t in range(count)]
    solved = []

    def whole(strip, i):
        return jnp.broadcast_to(strip[i:i + 1, :], (STRIP, BLK))

    def single(strip, at):
        return jnp.broadcast_to(strip[:, at:at + 1], (STRIP, BLK))

    here_strip = strips[0]
    cols = [single(here_strip, j) for j in span]
    for t in range(count):
        more = t + 1 < count
        here = (lane >= STRIP * t) & (lane < STRIP * (t + 1))
        here_strip = jnp.where(here, jnp.where(lane == STRIP * t + sublane, one, zero), here_strip)
        if more:
            pick = lane == STRIP * (t + 1) + sublane
            next_strip = jnp.where(here, zero, strips[t + 1])
            next_cols = [single(next_strip, STRIP * (t + 1) + j) for j in span]
            sum_strip, sum_cols = None, [None] * STRIP
        for k in span:
            scale = lax.rsqrt(whole(cols[k], k))
            factor = cols[k] * scale
            for j in range(k + 1, STRIP):
                cols[j] = cols[j] - factor * whole(factor, j)
            row = whole(here_strip, k) * scale
            below = jnp.where(sublane > k, factor, zero)
            here_strip = jnp.where(sublane == k, row, here_strip - below * row)
            if more:
                across = jnp.sum(jnp.where(pick, row, zero), axis=1, keepdims=True)
                across = jnp.broadcast_to(across, (STRIP, BLK))
                terms = [across * row] + [across * whole(across, j) for j in span]
                if k == 0:
                    sum_strip, sum_cols = terms[0], terms[1:]
                elif k < STRIP - 1:
                    sum_strip = sum_strip + terms[0]
                    sum_cols = [p + q for p, q in zip(sum_cols, terms[1:])]
                else:
                    next_strip = (next_strip - sum_strip) - terms[0]
                    next_cols = [(b - p) - q for b, p, q in zip(next_cols, sum_cols, terms[1:])]
        solved.append(here_strip)
        if more:
            last_strip = here_strip
            here_strip, cols = next_strip, next_cols
        if t + 2 < count:
            change = dot_tn(last_strip, last_strip)
            for s in range(t + 2, count):
                strips[s] = jnp.where(here, zero, strips[s]) - change[STRIP * s:STRIP * (s + 1), :]
    return jnp.concatenate(
        [jnp.where(lane < STRIP * (t + 1), solved[t], zero) for t in range(count)], axis=0)


def halves(x):
    high = x.astype(BF16)
    return high, (x - high.astype(F32)).astype(BF16)


def dot_nt3(lhs, rhs):
    def one(p, q):
        return lax.dot_general(p, q, (((1,), (1,)), ((), ())), preferred_element_type=F32)
    return one(lhs[0], rhs[0]) + (one(lhs[0], rhs[1]) + one(lhs[1], rhs[0]))


def dot_nn3(lhs, rhs):
    def one(p, q):
        return jnp.dot(p, q, preferred_element_type=F32)
    return one(lhs[0], rhs[0]) + (one(lhs[0], rhs[1]) + one(lhs[1], rhs[0]))


(SPREAD0, SPREAD1, SPREAD2, HEAD_A, HEAD_B, ACROSS_A, ACROSS_B, PAIR_A, PAIR_B, ROWS, ROWS_PAIR,
 ROWS_ON, SWAP, FIRST_Z, FIRST_Y, THEN_Y, THEN_Z, TILES) = range(18)
TURNED = TILES + 8
SEMS = TURNED + 4
L_SLAB, L_OWN, L_HEAD, L_ROWS, L_SWAP, L_IN, L_OUT, L_TURNED = 0, 1, 2, 3, 4, 5, 7, 9


def exchange_kernel(kr, out, panels, tiles, slab, head, work, diag, lower, whigh, wlow,
                    inbuf, high, low, obuf, turned, ssem, rsem, lsem):
    g = lax.axis_index("row")
    c = lax.axis_index("col")
    core = lax.rem(c, 2)
    other = (c // 2) * 2 + 1 - core
    y, z = g // 4, lax.rem(g, 4)
    swap_row = (g // 8) * 8 + c
    swap_col = lax.rem(g, 8)
    is_self = swap_col == c
    mine = pl.multiple_of(c * 64, 64)
    not_self = jnp.logical_not(is_self)
    chip = c // 2
    ahead = lax.rem(chip - swap_col // 2 + 4, 4)
    gives = ahead != 2

    def send(src, dst, index, row, col):
        pltpu.make_async_remote_copy(
            src_ref=src, dst_ref=dst, send_sem=ssem.at[index], recv_sem=rsem.at[index],
            device_id=(row, col), device_id_type=MESH).start()

    def local(src, dst, index):
        pltpu.make_async_copy(src, dst, lsem.at[index]).start()

    def done(ref, sem):
        pltpu.make_async_copy(ref, ref, sem).wait()

    local(kr.at[:, :, pl.ds(0, 1024)], slab, L_SLAB)
    for a in range(2):
        for b in range(4):
            at = pl.multiple_of((b * 8 + c) * 512, 512)
            local(kr.at[a, :, pl.ds(at, 512)], tiles.at[a * 4 + b, pl.ds(mine, 64), :], L_OWN)

    barrier = pltpu.get_barrier_semaphore()

    @pl.loop(1, 16)
    def _(o):
        pl.semaphore_signal(barrier, inc=1, device_id=(lax.rem(g + o, 16), c), device_id_type=MESH)

    @pl.loop(1, 8)
    def _(o):
        pl.semaphore_signal(barrier, inc=1, device_id=(g, lax.rem(c + o, 8)), device_id_type=MESH)

    @pl.when(not_self)
    def _():
        pl.semaphore_signal(barrier, inc=1, device_id=(swap_row, swap_col), device_id_type=MESH)

    for half in range(2):
        for o in range(-2, 4):
            src_row, src_col = c + 8 * half, lax.rem((c // 2) * 2 + o + 8, 8)

            @pl.when((src_row != g) | (src_col != c))
            def _():
                pl.semaphore_signal(barrier, inc=1, device_id=(src_row, src_col),
                                    device_id_type=MESH)

    pl.semaphore_wait(barrier, 22 + jnp.where(is_self, 15, 1 + jnp.where(gives, 16, 0)))

    done(slab, lsem.at[L_SLAB])

    def piece(which, q):
        return head.at[which, pl.ds(pl.multiple_of(mine + (q // 2) * 8, 8), 8),
                       pl.ds(pl.multiple_of(lax.rem(q, 2) * 256, 256), 256)]

    def spread(which, root, lanes_at, index):
        def src(q):
            return slab.at[0, pl.ds(pl.multiple_of((q // 2) * 8, 8), 8),
                           pl.ds(pl.multiple_of(lanes_at + lax.rem(q, 2) * 256, 256), 256)]

        @pl.when(g == root)
        def _():
            @pl.loop(1, 16)
            def _(o):
                q = lax.rem(g + o, 16)
                send(src(q), piece(which, q), index, q, c)
            local(src(g), piece(which, g), L_HEAD)

    spread(0, 0, 0, SPREAD0)
    spread(2, 1, 512, SPREAD2)
    spread(1, 0, 512, SPREAD1)

    def col_slab(a, r):
        return panels.at[2 + r // 8 + 2 * a, pl.ds(pl.multiple_of(lax.rem(r, 8) * 64, 64), 64), :]

    @pl.when(not_self)
    def _():
        for a in range(2):
            send(slab.at[a], col_slab(a, swap_row), SWAP, swap_row, swap_col)

    @pl.when(is_self)
    def _():
        for a in range(2):
            local(slab.at[a], col_slab(a, g), L_SWAP)

    def send_tiles(first, last):
        @pl.loop(first, last)
        def _(n):
            @pl.loop(1, 8)
            def _(o):
                cc = lax.rem(c + o, 8)
                at = pl.multiple_of((lax.rem(n, 4) * 8 + cc) * 512, 512)
                send(kr.at[n // 4, :, pl.ds(at, 512)], tiles.at[n, pl.ds(mine, 64), :],
                     TILES + n, g, cc)

    def lanes(group):
        return pl.ds(pl.multiple_of(group * BLK, BLK), BLK)

    def send_parts():
        @pl.loop(4, 8)
        def _(n):
            def part(cc, group):
                at = pl.multiple_of(((n - 4) * 8 + cc) * 512 + group * BLK, BLK)
                send(kr.at[1, :, pl.ds(at, BLK)], tiles.at[n, pl.ds(mine, 64), lanes(group)],
                     TILES + n, g, cc)

            at = pl.multiple_of(((n - 4) * 8 + other) * 512, 512)
            send(kr.at[1, :, pl.ds(at, 512)], tiles.at[n, pl.ds(mine, 64), :], TILES + n, g, other)
            for o in (1, 2, 3):
                there = lax.rem(chip + o, 4)
                for k in range(2):
                    if o == 2:
                        part(there * 2 + k, chip)
                    else:
                        for q in range(1, 4):
                            part(there * 2 + k, lax.rem(there + q, 4))

    def send_turned():
        home = swap_col // 2
        rows = pl.ds(pl.multiple_of(core * 64, 64), 64)

        def block(a, to, group):
            at = pl.multiple_of((16 + to) * 512 + group * BLK, BLK)
            return kr.at[a, :, pl.ds(at, BLK)]

        @pl.loop(0, 16)
        def _(o):
            to = lax.rem(g + o, 16)
            away = (to != g) | not_self
            for a in range(2):
                b = g // 8 + 2 * a
                for q in range(1, 4):
                    @pl.when((ahead == 0) & away)
                    def _():
                        send(block(a, to, lax.rem(home + q, 4)), turned.at[b, q - 1, rows, :],
                             TURNED + b, to, swap_col)

                    @pl.when((ahead == 0) & jnp.logical_not(away))
                    def _():
                        local(block(a, to, lax.rem(home + q, 4)), turned.at[b, q - 1, rows, :],
                              L_TURNED)
                for d, slot in ((1, 3), (3, 4)):
                    @pl.when(ahead == d)
                    def _():
                        send(block(a, to, lax.rem(home + 2, 4)), turned.at[b, slot, rows, :],
                             TURNED + b, to, swap_col)

    send_tiles(0, 1)

    def gather_head(which, index):
        @pl.loop(1, 16)
        def _(o):
            send(piece(which, g), piece(which, g), index, lax.rem(g + o, 16), c)

    def chunk(which, col):
        return head.at[which, pl.ds(pl.multiple_of(col * 64, 64), 64), :]

    def across(which, index):
        for o in range(1, 4):
            send(chunk(which, c), chunk(which, c), index, g, lax.rem(c + 2 * o, 8))

    def pair(which, index):
        for o in range(4):
            src = chunk(which, lax.rem(c + 2 * o, 8))
            send(src, src, index, g, other)

    @pl.when(g == 0)
    def _():
        done(head.at[0, pl.ds(0, 16), pl.ds(0, 256)], lsem.at[L_HEAD])

    @pl.when(g == 1)
    def _():
        done(head.at[0, pl.ds(0, 8), pl.ds(0, 256)], lsem.at[L_HEAD])

    @pl.when(g != 0)
    def _():
        done(piece(0, g), rsem.at[SPREAD0])

    gather_head(0, HEAD_A)

    @pl.when(g != 0)
    def _():
        done(piece(1, g), rsem.at[SPREAD1])

    @pl.when(g != 1)
    def _():
        done(piece(2, g), rsem.at[SPREAD2])

    gather_head(1, HEAD_B)
    gather_head(2, HEAD_B)
    done(head.at[0, pl.ds(0, 120), pl.ds(0, 256)], rsem.at[HEAD_A])
    across(0, ACROSS_A)

    @pl.when(not_self)
    def _():
        done(slab, rsem.at[SWAP])

    @pl.when(is_self)
    def _():
        done(slab, lsem.at[L_SWAP])

    def row_of(dy, dz):
        return lax.rem(y + dy, 4) * 4 + lax.rem(z + dz, 4)

    for o in range(1, 4):
        send(col_slab(0, g), col_slab(0, g), FIRST_Z, row_of(0, o), c)
        send(col_slab(1, g), col_slab(1, g), FIRST_Y, row_of(o, 0), c)

    done(head.at[1, pl.ds(0, 240), pl.ds(0, 256)], rsem.at[HEAD_B])
    across(1, ACROSS_B)
    across(2, ACROSS_B)

    for a in range(2):
        dst = panels.at[a, pl.ds(mine, 64), :]
        for o in range(1, 4):
            send(slab.at[a], dst, ROWS, g, lax.rem(c + 2 * o, 8))
        send(slab.at[a], dst, ROWS_PAIR, g, other)
        local(slab.at[a], dst, L_ROWS)

    send_tiles(1, 4)
    send_parts()
    done(head.at[0, pl.ds(0, 192), :], rsem.at[ACROSS_A])
    pair(0, PAIR_A)

    def second_stage():
        three = panels.at[0, pl.ds(0, 192), :]
        done(three, rsem.at[FIRST_Z])
        done(three, rsem.at[FIRST_Y])

        @pl.loop(0, 4)
        def _(n):
            from_z, from_y = row_of(0, n), row_of(n, 0)
            for o in range(1, 4):
                send(col_slab(0, from_z), col_slab(0, from_z), THEN_Y, row_of(o, 0), c)
                send(col_slab(1, from_y), col_slab(1, from_y), THEN_Z, row_of(0, o), c)

    def rows_on():
        done(panels.at[0, pl.ds(0, 384), :], rsem.at[ROWS])
        for a in range(2):
            for o in range(1, 4):
                at = pl.multiple_of(lax.rem(c + 2 * o, 8) * 64, 64)
                src = panels.at[a, pl.ds(at, 64), :]
                send(src, src, ROWS_ON, g, other)

    done(head.at[0, pl.ds(0, 256), :], rsem.at[PAIR_A])

    lane_blk = lax.broadcasted_iota(jnp.int32, (BLK, 512), 1) // BLK
    blocks = 512 // BLK
    upper = (lax.broadcasted_iota(jnp.int32, (BLK, BLK), 0)
             <= lax.broadcasted_iota(jnp.int32, (BLK, BLK), 1))

    def factor(panel, between):
        @pl.loop(0, blocks)
        def _(kb):
            at = pl.multiple_of(kb * BLK, BLK)
            inverse = factor_block(work[pl.ds(at, BLK), pl.ds(at, BLK)])
            work[pl.ds(at, BLK), :] = jnp.dot(inverse, work[pl.ds(at, BLK), :], precision=HI,
                                              preferred_element_type=F32)
            diag[kb] = jnp.where(upper, work[pl.ds(at, BLK), pl.ds(at, BLK)], F32(0.0))
            work[pl.ds(at, BLK), pl.ds(at, BLK)] = inverse

            @pl.loop(kb + 1, blocks)
            def _(rb):
                to = pl.multiple_of(rb * BLK, BLK)
                change = dot_tn(work[pl.ds(at, BLK), pl.ds(to, BLK)], work[pl.ds(at, BLK), :])
                old = work[pl.ds(to, BLK), :]
                work[pl.ds(to, BLK), :] = jnp.where(lane_blk == kb, F32(0.0), old) - change

            between(kb)

        for r in range(blocks):
            here = slice(r * BLK, (r + 1) * BLK)
            row = jnp.where(lane_blk <= r, work[here, :], F32(0.0))
            whigh[2 * panel, here, :], wlow[2 * panel, here, :] = halves(row)
            for s in range(blocks):
                there = slice(s * BLK, (s + 1) * BLK)
                if s > r:
                    lower[2 * panel, here, there] = jnp.zeros((BLK, BLK), F32)
                elif s == r:
                    lower[2 * panel, here, there] = diag[r].T
                else:
                    lower[2 * panel, here, there] = work[there, here].T

    work[...] = head[0]

    def between(kb):
        @pl.when(kb == 0)
        def _():
            second_stage()

        @pl.when(kb == 1)
        def _():
            done(head.at[1, pl.ds(0, 384), :], rsem.at[ACROSS_B])
            pair(1, PAIR_B)
            pair(2, PAIR_B)

        @pl.when(kb == 2)
        def _():
            send_turned()

        @pl.when(kb == 3)
        def _():
            rows_on()

    factor(0, between)
    done(head.at[pl.ds(1, 2), pl.ds(0, 256), :], rsem.at[PAIR_B])

    right = dot_nn3((whigh[0], wlow[0]), halves(head[1]))
    whigh[1], wlow[1] = halves(right)
    lower[1] = right.T
    work[...] = head[2] - dot_tn(right, right)
    factor(1, lambda kb: None)

    done(panels.at[0, pl.ds(0, 128), :], rsem.at[ROWS_PAIR])
    done(panels.at[0, pl.ds(0, 384), :], rsem.at[ROWS_ON])
    done(slab, lsem.at[L_ROWS])
    twelve = panels.at[pl.ds(0, 2), pl.ds(0, 384), :]

    def fetch(t, slot):
        return pltpu.make_async_copy(panels.at[t], inbuf.at[slot], lsem.at[L_IN + slot])

    fetch(0, 0).start()

    @pl.loop(0, 6)
    def _(t):
        slot = lax.rem(t, 2)

        @pl.when(t == 1)
        def _():
            done(twelve, rsem.at[THEN_Y])
            done(twelve, rsem.at[THEN_Z])

        @pl.when(t < 5)
        def _():
            fetch(t + 1, 1 - slot).start()

        fetch(t, slot).wait()
        first = dot_nt3(halves(inbuf[slot, :, :512]), (whigh[0], wlow[0]))
        top, rest = halves(first)
        high[t, :, :512], low[t, :, :512] = top, rest
        left = inbuf[slot, :, 512:] - dot_nn3((top, rest), (whigh[1], wlow[1]))
        high[t, :, 512:], low[t, :, 512:] = halves(dot_nt3(halves(left), (whigh[2], wlow[2])))

    done(tiles.at[0], lsem.at[L_OWN])

    @pl.when(is_self)
    def _():
        done(tiles.at[0, pl.ds(0, 96), :], lsem.at[L_TURNED])

    def turn(n):
        b = n - 4
        own_source = is_self & (lax.rem(b, 2) == g // 8)

        @pl.when(own_source)
        def _():
            done(tiles.at[0, pl.ds(0, 112), :], rsem.at[TURNED + b])

        @pl.when(jnp.logical_not(own_source))
        def _():
            done(turned.at[b], rsem.at[TURNED + b])

        places = ((1, 0), (2, 0), (3, 0), (2, 1), (2, 3))
        for slot, (down, right) in enumerate(places):
            tiles[n, lanes(lax.rem(chip + down, 4)), lanes(lax.rem(chip + right, 4))] = (
                turned[b, slot].T)

    def leave(pair_no, slot):
        at = pl.multiple_of(lax.rem(pair_no, 2) * 8, 8)
        return pltpu.make_async_copy(
            obuf.at[slot], out.at[pair_no // 2, :, pl.ds(at, 8), :], lsem.at[L_OUT + slot])

    @pl.loop(0, 8)
    def _(n):
        a, b = n // 4, lax.rem(n, 4)
        pair_no = n // 2
        slot = lax.rem(pair_no, 2)
        half = lax.rem(n, 2)
        flat = obuf.at[slot].reshape(512 * 8, 128)

        def put(value):
            for m in range(4):
                flat[pl.ds(half * 4 + m, 512, stride=8), :] = value[:, m * 128:(m + 1) * 128]

        @pl.when((half == 0) & (pair_no >= 2))
        def _():
            leave(pair_no - 2, slot).wait()

        @pl.when(n < 4)
        def _():
            done(tiles.at[n, pl.ds(0, 448), :], rsem.at[TILES + n])

        @pl.when(n >= 4)
        def _():
            done(tiles.at[n, pl.ds(0, 288), :], rsem.at[TILES + n])
            turn(n)

        special_row = (a == 0) & (g < 2)
        special_col = (b == 0) & (c < 2)

        @pl.when(jnp.logical_not(special_row | special_col))
        def _():
            put(tiles[n] - dot_nt3((high[a], low[a]), (high[2 + b], low[2 + b])))

        @pl.when(special_col & jnp.logical_not(special_row) & (c == 0))
        def _():
            put(high[a, :, :512].astype(F32) + low[a, :, :512].astype(F32))

        @pl.when(special_col & jnp.logical_not(special_row) & (c == 1))
        def _():
            put(high[a, :, 512:].astype(F32) + low[a, :, 512:].astype(F32))

        for corner in range(3):
            @pl.when(special_row & (b == 0) & (c <= g) & (g + c == corner))
            def _():
                put(lower[corner])

        @pl.when(special_row & ((b > 0) | (c > g)))
        def _():
            put(jnp.zeros((512, 512), F32))

        @pl.when(half == 1)
        def _():
            leave(pair_no, slot).start()

    for pair_no in range(2, 4):
        leave(pair_no, pair_no % 2).wait()

    @pl.loop(0, 4)
    def _(n):
        done(tiles.at[n, pl.ds(0, 448), :], ssem.at[TILES + n])
        done(tiles.at[n, pl.ds(0, 288), :], ssem.at[TILES + 4 + n])

    for a in range(2):
        index = TURNED + g // 8 + 2 * a

        @pl.when((ahead == 0) & not_self)
        def _():
            done(tiles.at[pl.ds(0, 3), pl.ds(0, 256), :], ssem.at[index])

        @pl.when(is_self)
        def _():
            done(tiles.at[pl.ds(0, 3), pl.ds(0, 240), :], ssem.at[index])

        @pl.when((ahead == 1) | (ahead == 3))
        def _():
            done(tiles.at[0, pl.ds(0, 256), :], ssem.at[index])

    @pl.when(g == 0)
    def _():
        done(head.at[0, pl.ds(0, 120), pl.ds(0, 256)], ssem.at[SPREAD0])
        done(head.at[0, pl.ds(0, 120), pl.ds(0, 256)], ssem.at[SPREAD1])

    @pl.when(g == 1)
    def _():
        done(head.at[0, pl.ds(0, 120), pl.ds(0, 256)], ssem.at[SPREAD2])

    done(head.at[0, pl.ds(0, 120), pl.ds(0, 256)], ssem.at[HEAD_A])
    done(head.at[1, pl.ds(0, 240), pl.ds(0, 256)], ssem.at[HEAD_B])
    done(head.at[0, pl.ds(0, 192), :], ssem.at[ACROSS_A])
    done(head.at[1, pl.ds(0, 384), :], ssem.at[ACROSS_B])
    done(head.at[0, pl.ds(0, 256), :], ssem.at[PAIR_A])
    done(head.at[pl.ds(1, 2), pl.ds(0, 256), :], ssem.at[PAIR_B])
    done(panels.at[0, pl.ds(0, 384), :], ssem.at[ROWS])
    done(panels.at[0, pl.ds(0, 128), :], ssem.at[ROWS_PAIR])
    done(panels.at[0, pl.ds(0, 384), :], ssem.at[ROWS_ON])

    @pl.when(not_self)
    def _():
        done(slab, ssem.at[SWAP])

    three = panels.at[0, pl.ds(0, 192), :]
    done(three, ssem.at[FIRST_Z])
    done(three, ssem.at[FIRST_Y])
    done(twelve, ssem.at[THEN_Y])
    done(twelve, ssem.at[THEN_Z])


def exchange(rows):
    anyspace = pl.BlockSpec(memory_space=pl.ANY)
    return pl.pallas_call(
        exchange_kernel,
        out_shape=(
            jax.ShapeDtypeStruct((2, 512, 16, 128), F32),
            jax.ShapeDtypeStruct((6, 512, 1024), F32),
        ),
        in_specs=[anyspace],
        out_specs=(anyspace,) * 2,
        scratch_shapes=[
            pltpu.VMEM((8, 512, 512), F32),
            pltpu.VMEM((2, 64, 1024), F32),
            pltpu.VMEM((3, 512, 512), F32),
            pltpu.VMEM((512, 512), F32),
            pltpu.VMEM((4, BLK, BLK), F32),
            pltpu.VMEM((3, 512, 512), F32),
            pltpu.VMEM((3, 512, 512), BF16),
            pltpu.VMEM((3, 512, 512), BF16),
            pltpu.VMEM((2, 512, 1024), F32),
            pltpu.VMEM((6, 512, 1024), BF16),
            pltpu.VMEM((6, 512, 1024), BF16),
            pltpu.VMEM((2, 512, 8, 128), F32),
            pltpu.VMEM((4, 5, BLK, BLK), F32),
            pltpu.SemaphoreType.DMA((SEMS,)),
            pltpu.SemaphoreType.DMA((SEMS,)),
            pltpu.SemaphoreType.DMA((10,)),
        ],
        compiler_params=pltpu.CompilerParams(
            collective_id=1, has_side_effects=True, vmem_limit_bytes=56 * 1024 * 1024),
        name="exchange",
    )(rows)


def shards(kernel_rows):
    rows = kernel_rows.reshape(2, 64, 16384)
    out, _ = exchange(rows)
    return out.reshape(2, 1, 512, 4, 1, 512)


def solution(mesh):
    return jax.shard_map(
        shards,
        mesh=mesh,
        in_specs=(P(None, "row", "col", None, None),),
        out_specs=P(None, "row", None, None, "col", None),
        check_vma=False,
    )
```

```python
import functools
import jax
import jax.numpy as jnp
from jax import lax
from jax.experimental import pallas as pl
from jax.experimental.pallas import tpu as pltpu
from jax.sharding import PartitionSpec as P

MESH = pl.DeviceIdType.MESH
HI = lax.Precision.HIGHEST
F32 = jnp.float32
BF16 = jnp.bfloat16
BLK = 128
STRIP = 8


def dot_tn(lhs, rhs):
    return lax.dot_general(lhs, rhs, (((0,), (0,)), ((), ())), precision=HI,
                           preferred_element_type=F32)


def factor_block(block):
    count = BLK // STRIP
    lane = lax.broadcasted_iota(jnp.int32, (STRIP, BLK), 1)
    sublane = lax.broadcasted_iota(jnp.int32, (STRIP, BLK), 0)
    zero, one = F32(0.0), F32(1.0)
    span = range(STRIP)
    strips = [block[STRIP * t:STRIP * (t + 1), :] for t in range(count)]
    solved = []

    def whole(strip, i):
        return jnp.broadcast_to(strip[i:i + 1, :], (STRIP, BLK))

    def single(strip, at):
        return jnp.broadcast_to(strip[:, at:at + 1], (STRIP, BLK))

    here_strip = strips[0]
    cols = [single(here_strip, j) for j in span]
    for t in range(count):
        more = t + 1 < count
        here = (lane >= STRIP * t) & (lane < STRIP * (t + 1))
        here_strip = jnp.where(here, jnp.where(lane == STRIP * t + sublane, one, zero), here_strip)
        if more:
            pick = lane == STRIP * (t + 1) + sublane
            next_strip = jnp.where(here, zero, strips[t + 1])
            next_cols = [single(next_strip, STRIP * (t + 1) + j) for j in span]
            sum_strip, sum_cols = None, [None] * STRIP
        for k in span:
            scale = lax.rsqrt(whole(cols[k], k))
            factor = cols[k] * scale
            for j in range(k + 1, STRIP):
                cols[j] = cols[j] - factor * whole(factor, j)
            row = whole(here_strip, k) * scale
            below = jnp.where(sublane > k, factor, zero)
            here_strip = jnp.where(sublane == k, row, here_strip - below * row)
            if more:
                across = jnp.sum(jnp.where(pick, row, zero), axis=1, keepdims=True)
                across = jnp.broadcast_to(across, (STRIP, BLK))
                terms = [across * row] + [across * whole(across, j) for j in span]
                if k == 0:
                    sum_strip, sum_cols = terms[0], terms[1:]
                elif k < STRIP - 1:
                    sum_strip = sum_strip + terms[0]
                    sum_cols = [p + q for p, q in zip(sum_cols, terms[1:])]
                else:
                    next_strip = (next_strip - sum_strip) - terms[0]
                    next_cols = [(b - p) - q for b, p, q in zip(next_cols, sum_cols, terms[1:])]
        solved.append(here_strip)
        if more:
            last_strip = here_strip
            here_strip, cols = next_strip, next_cols
        if t + 2 < count:
            change = dot_tn(last_strip, last_strip)
            for s in range(t + 2, count):
                strips[s] = jnp.where(here, zero, strips[s]) - change[STRIP * s:STRIP * (s + 1), :]
    return jnp.concatenate(
        [jnp.where(lane < STRIP * (t + 1), solved[t], zero) for t in range(count)], axis=0)


def halves(x):
    high = x.astype(BF16)
    return high, (x - high.astype(F32)).astype(BF16)


def dot_nt3(lhs, rhs):
    def one(p, q):
        return lax.dot_general(p, q, (((1,), (1,)), ((), ())), preferred_element_type=F32)
    return one(lhs[0], rhs[0]) + (one(lhs[0], rhs[1]) + one(lhs[1], rhs[0]))


def dot_nn3(lhs, rhs):
    def one(p, q):
        return jnp.dot(p, q, preferred_element_type=F32)
    return one(lhs[0], rhs[0]) + (one(lhs[0], rhs[1]) + one(lhs[1], rhs[0]))


(SPREAD0, SPREAD1, SPREAD2, HEAD_A, HEAD_B, ACROSS_A, ACROSS_B, PAIR_A, PAIR_B, ROWS, ROWS_PAIR,
 ROWS_ON, SWAP, FIRST_Z, FIRST_Y, THEN_Y, THEN_Z, TILES) = range(18)
TURNED = TILES + 8
SEMS = TURNED + 8
L_SLAB, L_OWN, L_HEAD, L_ROWS, L_SWAP, L_IN, L_OUT, L_TURNED = 0, 1, 2, 3, 4, 5, 7, 9


def exchange_kernel(kr, out, panels, tiles, slab, head, work, diag, lower, whigh, wlow,
                    inbuf, high, low, obuf, turned, ssem, rsem, lsem):
    g = lax.axis_index("row")
    c = lax.axis_index("col")
    core = lax.rem(c, 2)
    other = (c // 2) * 2 + 1 - core
    y, z = g // 4, lax.rem(g, 4)
    swap_row = (g // 8) * 8 + c
    swap_col = lax.rem(g, 8)
    is_self = swap_col == c
    mine = pl.multiple_of(c * 64, 64)
    not_self = jnp.logical_not(is_self)
    chip = c // 2
    gives = chip == swap_col // 2

    def send(src, dst, index, row, col):
        pltpu.make_async_remote_copy(
            src_ref=src, dst_ref=dst, send_sem=ssem.at[index], recv_sem=rsem.at[index],
            device_id=(row, col), device_id_type=MESH).start()

    def local(src, dst, index):
        pltpu.make_async_copy(src, dst, lsem.at[index]).start()

    def done(ref, sem):
        pltpu.make_async_copy(ref, ref, sem).wait()

    local(kr.at[:, :, pl.ds(0, 1024)], slab, L_SLAB)
    for a in range(2):
        for b in range(4):
            at = pl.multiple_of((b * 8 + c) * 512, 512)
            local(kr.at[a, :, pl.ds(at, 512)], tiles.at[a * 4 + b, pl.ds(mine, 64), :], L_OWN)

    barrier = pltpu.get_barrier_semaphore()

    @pl.loop(1, 16)
    def _(o):
        pl.semaphore_signal(barrier, inc=1, device_id=(lax.rem(g + o, 16), c), device_id_type=MESH)

    @pl.loop(1, 8)
    def _(o):
        pl.semaphore_signal(barrier, inc=1, device_id=(g, lax.rem(c + o, 8)), device_id_type=MESH)

    @pl.when(not_self)
    def _():
        pl.semaphore_signal(barrier, inc=1, device_id=(swap_row, swap_col), device_id_type=MESH)

    for half in range(2):
        for o in range(2):
            src_row, src_col = c + 8 * half, chip * 2 + o

            @pl.when((src_row != g) | (src_col != c))
            def _():
                pl.semaphore_signal(barrier, inc=1, device_id=(src_row, src_col),
                                    device_id_type=MESH)

    pl.semaphore_wait(barrier, 22 + jnp.where(is_self, 15, 1 + jnp.where(gives, 16, 0)))

    done(slab, lsem.at[L_SLAB])

    def piece(which, q):
        return head.at[which, pl.ds(pl.multiple_of(mine + (q // 2) * 8, 8), 8),
                       pl.ds(pl.multiple_of(lax.rem(q, 2) * 256, 256), 256)]

    def spread(which, root, lanes_at, index):
        def src(q):
            return slab.at[0, pl.ds(pl.multiple_of((q // 2) * 8, 8), 8),
                           pl.ds(pl.multiple_of(lanes_at + lax.rem(q, 2) * 256, 256), 256)]

        @pl.when(g == root)
        def _():
            @pl.loop(1, 16)
            def _(o):
                q = lax.rem(g + o, 16)
                send(src(q), piece(which, q), index, q, c)
            local(src(g), piece(which, g), L_HEAD)

    spread(0, 0, 0, SPREAD0)
    spread(2, 1, 512, SPREAD2)
    spread(1, 0, 512, SPREAD1)

    def col_slab(a, r):
        return panels.at[2 + r // 8 + 2 * a, pl.ds(pl.multiple_of(lax.rem(r, 8) * 64, 64), 64), :]

    @pl.when(not_self)
    def _():
        for a in range(2):
            send(slab.at[a], col_slab(a, swap_row), SWAP, swap_row, swap_col)

    @pl.when(is_self)
    def _():
        for a in range(2):
            local(slab.at[a], col_slab(a, g), L_SWAP)

    def lanes(group):
        return pl.ds(pl.multiple_of(group * BLK, BLK), BLK)

    def send_parts(first, last):
        @pl.loop(first, last)
        def _(n):
            a, b = n // 4, lax.rem(n, 4)

            def whole(cc):
                at = pl.multiple_of((b * 8 + cc) * 512, 512)
                send(kr.at[a, :, pl.ds(at, 512)], tiles.at[n, pl.ds(mine, 64), :],
                     TILES + n, g, cc)

            whole(other)
            for k in range(2):
                whole(lax.rem(chip + 1, 4) * 2 + k)
                whole(lax.rem(chip + 3, 4) * 2 + k)
            there = lax.rem(chip + 2, 4)
            for k in range(2):
                for q in range(1, 4):
                    group = lax.rem(there + q, 4)
                    at = pl.multiple_of((b * 8 + there * 2 + k) * 512 + group * BLK, BLK)
                    send(kr.at[a, :, pl.ds(at, BLK)], tiles.at[n, pl.ds(mine, 64), lanes(group)],
                         TILES + n, g, there * 2 + k)

    def send_turned(first, last):
        far = lax.rem(swap_col // 2 + 2, 4)
        rows = pl.ds(pl.multiple_of(core * 64, 64), 64)

        @pl.when(gives)
        def _():
            @pl.loop(0, 16)
            def _(o):
                to = lax.rem(g + o, 16)
                away = (to != g) | not_self
                for dest_a in range(first, last):
                    for a in range(2):
                        n = dest_a * 4 + g // 8 + 2 * a
                        at = pl.multiple_of((dest_a * 16 + to) * 512 + far * BLK, BLK)
                        src = kr.at[a, :, pl.ds(at, BLK)]
                        dst = turned.at[n, rows, :]

                        @pl.when(away)
                        def _():
                            send(src, dst, TURNED + n, to, swap_col)

                        @pl.when(jnp.logical_not(away))
                        def _():
                            local(src, dst, L_TURNED)

    send_parts(0, 1)

    def gather_head(which, index):
        @pl.loop(1, 16)
        def _(o):
            send(piece(which, g), piece(which, g), index, lax.rem(g + o, 16), c)

    def chunk(which, col):
        return head.at[which, pl.ds(pl.multiple_of(col * 64, 64), 64), :]

    def across(which, index):
        for o in range(1, 4):
            send(chunk(which, c), chunk(which, c), index, g, lax.rem(c + 2 * o, 8))

    def pair(which, index):
        for o in range(4):
            src = chunk(which, lax.rem(c + 2 * o, 8))
            send(src, src, index, g, other)

    @pl.when(g == 0)
    def _():
        done(head.at[0, pl.ds(0, 16), pl.ds(0, 256)], lsem.at[L_HEAD])

    @pl.when(g == 1)
    def _():
        done(head.at[0, pl.ds(0, 8), pl.ds(0, 256)], lsem.at[L_HEAD])

    @pl.when(g != 0)
    def _():
        done(piece(0, g), rsem.at[SPREAD0])

    gather_head(0, HEAD_A)

    @pl.when(g != 0)
    def _():
        done(piece(1, g), rsem.at[SPREAD1])

    @pl.when(g != 1)
    def _():
        done(piece(2, g), rsem.at[SPREAD2])

    gather_head(1, HEAD_B)
    gather_head(2, HEAD_B)
    done(head.at[0, pl.ds(0, 120), pl.ds(0, 256)], rsem.at[HEAD_A])
    across(0, ACROSS_A)

    @pl.when(not_self)
    def _():
        done(slab, rsem.at[SWAP])

    @pl.when(is_self)
    def _():
        done(slab, lsem.at[L_SWAP])

    def row_of(dy, dz):
        return lax.rem(y + dy, 4) * 4 + lax.rem(z + dz, 4)

    for o in range(1, 4):
        send(col_slab(0, g), col_slab(0, g), FIRST_Z, row_of(0, o), c)
        send(col_slab(1, g), col_slab(1, g), FIRST_Y, row_of(o, 0), c)

    done(head.at[1, pl.ds(0, 240), pl.ds(0, 256)], rsem.at[HEAD_B])
    across(1, ACROSS_B)
    across(2, ACROSS_B)

    for a in range(2):
        dst = panels.at[a, pl.ds(mine, 64), :]
        for o in range(1, 4):
            send(slab.at[a], dst, ROWS, g, lax.rem(c + 2 * o, 8))
        send(slab.at[a], dst, ROWS_PAIR, g, other)
        local(slab.at[a], dst, L_ROWS)

    send_parts(1, 8)
    done(head.at[0, pl.ds(0, 192), :], rsem.at[ACROSS_A])
    pair(0, PAIR_A)

    def second_stage():
        three = panels.at[0, pl.ds(0, 192), :]
        done(three, rsem.at[FIRST_Z])
        done(three, rsem.at[FIRST_Y])

        @pl.loop(0, 4)
        def _(n):
            from_z, from_y = row_of(0, n), row_of(n, 0)
            for o in range(1, 4):
                send(col_slab(0, from_z), col_slab(0, from_z), THEN_Y, row_of(o, 0), c)
                send(col_slab(1, from_y), col_slab(1, from_y), THEN_Z, row_of(0, o), c)

    def rows_on():
        done(panels.at[0, pl.ds(0, 384), :], rsem.at[ROWS])
        for a in range(2):
            for o in range(1, 4):
                at = pl.multiple_of(lax.rem(c + 2 * o, 8) * 64, 64)
                src = panels.at[a, pl.ds(at, 64), :]
                send(src, src, ROWS_ON, g, other)

    done(head.at[0, pl.ds(0, 256), :], rsem.at[PAIR_A])

    lane_blk = lax.broadcasted_iota(jnp.int32, (BLK, 512), 1) // BLK
    blocks = 512 // BLK
    upper = (lax.broadcasted_iota(jnp.int32, (BLK, BLK), 0)
             <= lax.broadcasted_iota(jnp.int32, (BLK, BLK), 1))

    def factor(panel, between):
        @pl.loop(0, blocks)
        def _(kb):
            at = pl.multiple_of(kb * BLK, BLK)
            inverse = factor_block(work[pl.ds(at, BLK), pl.ds(at, BLK)])
            work[pl.ds(at, BLK), :] = jnp.dot(inverse, work[pl.ds(at, BLK), :], precision=HI,
                                              preferred_element_type=F32)
            diag[kb] = jnp.where(upper, work[pl.ds(at, BLK), pl.ds(at, BLK)], F32(0.0))
            work[pl.ds(at, BLK), pl.ds(at, BLK)] = inverse

            @pl.loop(kb + 1, blocks)
            def _(rb):
                to = pl.multiple_of(rb * BLK, BLK)
                change = dot_tn(work[pl.ds(at, BLK), pl.ds(to, BLK)], work[pl.ds(at, BLK), :])
                old = work[pl.ds(to, BLK), :]
                work[pl.ds(to, BLK), :] = jnp.where(lane_blk == kb, F32(0.0), old) - change

            between(kb)

        for r in range(blocks):
            here = slice(r * BLK, (r + 1) * BLK)
            row = jnp.where(lane_blk <= r, work[here, :], F32(0.0))
            whigh[2 * panel, here, :], wlow[2 * panel, here, :] = halves(row)
            for s in range(blocks):
                there = slice(s * BLK, (s + 1) * BLK)
                if s > r:
                    lower[2 * panel, here, there] = jnp.zeros((BLK, BLK), F32)
                elif s == r:
                    lower[2 * panel, here, there] = diag[r].T
                else:
                    lower[2 * panel, here, there] = work[there, here].T

    work[...] = head[0]

    def between(kb):
        @pl.when(kb == 0)
        def _():
            second_stage()

        @pl.when(kb == 1)
        def _():
            done(head.at[1, pl.ds(0, 384), :], rsem.at[ACROSS_B])
            pair(1, PAIR_B)
            pair(2, PAIR_B)

        @pl.when(kb == 2)
        def _():
            send_turned(0, 2)

        @pl.when(kb == 3)
        def _():
            rows_on()

    factor(0, between)
    done(head.at[pl.ds(1, 2), pl.ds(0, 256), :], rsem.at[PAIR_B])

    right = dot_nn3((whigh[0], wlow[0]), halves(head[1]))
    whigh[1], wlow[1] = halves(right)
    lower[1] = right.T
    work[...] = head[2] - dot_tn(right, right)
    factor(1, lambda kb: None)

    done(panels.at[0, pl.ds(0, 128), :], rsem.at[ROWS_PAIR])
    done(panels.at[0, pl.ds(0, 384), :], rsem.at[ROWS_ON])
    done(slab, lsem.at[L_ROWS])
    twelve = panels.at[pl.ds(0, 2), pl.ds(0, 384), :]

    def fetch(t, slot):
        return pltpu.make_async_copy(panels.at[t], inbuf.at[slot], lsem.at[L_IN + slot])

    fetch(0, 0).start()

    @pl.loop(0, 6)
    def _(t):
        slot = lax.rem(t, 2)

        @pl.when(t == 1)
        def _():
            done(twelve, rsem.at[THEN_Y])
            done(twelve, rsem.at[THEN_Z])

        @pl.when(t < 5)
        def _():
            fetch(t + 1, 1 - slot).start()

        fetch(t, slot).wait()
        first = dot_nt3(halves(inbuf[slot, :, :512]), (whigh[0], wlow[0]))
        top, rest = halves(first)
        high[t, :, :512], low[t, :, :512] = top, rest
        left = inbuf[slot, :, 512:] - dot_nn3((top, rest), (whigh[1], wlow[1]))
        high[t, :, 512:], low[t, :, 512:] = halves(dot_nt3(halves(left), (whigh[2], wlow[2])))

    done(tiles.at[0], lsem.at[L_OWN])

    @pl.when(is_self)
    def _():
        done(tiles.at[0, pl.ds(0, 64), :], lsem.at[L_TURNED])

    def turn(n):
        own_source = is_self & (lax.rem(n, 2) == g // 8)

        @pl.when(own_source)
        def _():
            done(tiles.at[0, pl.ds(0, 16), :], rsem.at[TURNED + n])

        @pl.when(jnp.logical_not(own_source))
        def _():
            done(turned.at[n], rsem.at[TURNED + n])

        tiles[n, lanes(lax.rem(chip + 2, 4)), lanes(chip)] = turned[n].T

    def leave(pair_no, slot):
        at = pl.multiple_of(lax.rem(pair_no, 2) * 8, 8)
        return pltpu.make_async_copy(
            obuf.at[slot], out.at[pair_no // 2, :, pl.ds(at, 8), :], lsem.at[L_OUT + slot])

    @pl.loop(0, 8)
    def _(n):
        a, b = n // 4, lax.rem(n, 4)
        pair_no = n // 2
        slot = lax.rem(pair_no, 2)
        half = lax.rem(n, 2)
        flat = obuf.at[slot].reshape(512 * 8, 128)

        def put(value):
            for m in range(4):
                flat[pl.ds(half * 4 + m, 512, stride=8), :] = value[:, m * 128:(m + 1) * 128]

        @pl.when((half == 0) & (pair_no >= 2))
        def _():
            leave(pair_no - 2, slot).wait()

        done(tiles.at[n, pl.ds(0, 416), :], rsem.at[TILES + n])
        turn(n)
        special_row = (a == 0) & (g < 2)
        special_col = (b == 0) & (c < 2)

        @pl.when(jnp.logical_not(special_row | special_col))
        def _():
            put(tiles[n] - dot_nt3((high[a], low[a]), (high[2 + b], low[2 + b])))

        @pl.when(special_col & jnp.logical_not(special_row) & (c == 0))
        def _():
            put(high[a, :, :512].astype(F32) + low[a, :, :512].astype(F32))

        @pl.when(special_col & jnp.logical_not(special_row) & (c == 1))
        def _():
            put(high[a, :, 512:].astype(F32) + low[a, :, 512:].astype(F32))

        for corner in range(3):
            @pl.when(special_row & (b == 0) & (c <= g) & (g + c == corner))
            def _():
                put(lower[corner])

        @pl.when(special_row & ((b > 0) | (c > g)))
        def _():
            put(jnp.zeros((512, 512), F32))

        @pl.when(half == 1)
        def _():
            leave(pair_no, slot).start()

    for pair_no in range(2, 4):
        leave(pair_no, pair_no % 2).wait()

    @pl.loop(0, 8)
    def _(n):
        done(tiles.at[n, pl.ds(0, 416), :], ssem.at[TILES + n])

    for dest_a in range(0, 2):
        for a in range(2):
            index = TURNED + dest_a * 4 + g // 8 + 2 * a

            @pl.when(gives & not_self)
            def _():
                done(tiles.at[0, pl.ds(0, 256), :], ssem.at[index])

            @pl.when(is_self)
            def _():
                done(tiles.at[0, pl.ds(0, 240), :], ssem.at[index])

    @pl.when(g == 0)
    def _():
        done(head.at[0, pl.ds(0, 120), pl.ds(0, 256)], ssem.at[SPREAD0])
        done(head.at[0, pl.ds(0, 120), pl.ds(0, 256)], ssem.at[SPREAD1])

    @pl.when(g == 1)
    def _():
        done(head.at[0, pl.ds(0, 120), pl.ds(0, 256)], ssem.at[SPREAD2])

    done(head.at[0, pl.ds(0, 120), pl.ds(0, 256)], ssem.at[HEAD_A])
    done(head.at[1, pl.ds(0, 240), pl.ds(0, 256)], ssem.at[HEAD_B])
    done(head.at[0, pl.ds(0, 192), :], ssem.at[ACROSS_A])
    done(head.at[1, pl.ds(0, 384), :], ssem.at[ACROSS_B])
    done(head.at[0, pl.ds(0, 256), :], ssem.at[PAIR_A])
    done(head.at[pl.ds(1, 2), pl.ds(0, 256), :], ssem.at[PAIR_B])
    done(panels.at[0, pl.ds(0, 384), :], ssem.at[ROWS])
    done(panels.at[0, pl.ds(0, 128), :], ssem.at[ROWS_PAIR])
    done(panels.at[0, pl.ds(0, 384), :], ssem.at[ROWS_ON])

    @pl.when(not_self)
    def _():
        done(slab, ssem.at[SWAP])

    three = panels.at[0, pl.ds(0, 192), :]
    done(three, ssem.at[FIRST_Z])
    done(three, ssem.at[FIRST_Y])
    done(twelve, ssem.at[THEN_Y])
    done(twelve, ssem.at[THEN_Z])


def exchange(rows):
    anyspace = pl.BlockSpec(memory_space=pl.ANY)
    return pl.pallas_call(
        exchange_kernel,
        out_shape=(
            jax.ShapeDtypeStruct((2, 512, 16, 128), F32),
            jax.ShapeDtypeStruct((6, 512, 1024), F32),
        ),
        in_specs=[anyspace],
        out_specs=(anyspace,) * 2,
        scratch_shapes=[
            pltpu.VMEM((8, 512, 512), F32),
            pltpu.VMEM((2, 64, 1024), F32),
            pltpu.VMEM((3, 512, 512), F32),
            pltpu.VMEM((512, 512), F32),
            pltpu.VMEM((4, BLK, BLK), F32),
            pltpu.VMEM((3, 512, 512), F32),
            pltpu.VMEM((3, 512, 512), BF16),
            pltpu.VMEM((3, 512, 512), BF16),
            pltpu.VMEM((2, 512, 1024), F32),
            pltpu.VMEM((6, 512, 1024), BF16),
            pltpu.VMEM((6, 512, 1024), BF16),
            pltpu.VMEM((2, 512, 8, 128), F32),
            pltpu.VMEM((8, BLK, BLK), F32),
            pltpu.SemaphoreType.DMA((SEMS,)),
            pltpu.SemaphoreType.DMA((SEMS,)),
            pltpu.SemaphoreType.DMA((10,)),
        ],
        compiler_params=pltpu.CompilerParams(
            collective_id=1, has_side_effects=True, vmem_limit_bytes=56 * 1024 * 1024),
        name="exchange",
    )(rows)


def shards(kernel_rows):
    rows = kernel_rows.reshape(2, 64, 16384)
    out, _ = exchange(rows)
    return out.reshape(2, 1, 512, 4, 1, 512)


def solution(mesh):
    return jax.shard_map(
        shards,
        mesh=mesh,
        in_specs=(P(None, "row", "col", None, None),),
        out_specs=P(None, "row", None, None, "col", None),
        check_vma=False,
    )
```

```python
import functools
import jax
import jax.numpy as jnp
from jax import lax
from jax.experimental import pallas as pl
from jax.experimental.pallas import tpu as pltpu
from jax.sharding import PartitionSpec as P

MESH = pl.DeviceIdType.MESH
HI = lax.Precision.HIGHEST
F32 = jnp.float32
BF16 = jnp.bfloat16
BLK = 128
STRIP = 8


def dot_tn(lhs, rhs):
    return lax.dot_general(lhs, rhs, (((0,), (0,)), ((), ())), precision=HI,
                           preferred_element_type=F32)


def factor_block(block):
    count = BLK // STRIP
    lane = lax.broadcasted_iota(jnp.int32, (STRIP, BLK), 1)
    sublane = lax.broadcasted_iota(jnp.int32, (STRIP, BLK), 0)
    zero, one = F32(0.0), F32(1.0)
    span = range(STRIP)
    strips = [block[STRIP * t:STRIP * (t + 1), :] for t in range(count)]
    solved = []

    def whole(strip, i):
        return jnp.broadcast_to(strip[i:i + 1, :], (STRIP, BLK))

    def single(strip, at):
        return jnp.broadcast_to(strip[:, at:at + 1], (STRIP, BLK))

    here_strip = strips[0]
    cols = [single(here_strip, j) for j in span]
    for t in range(count):
        more = t + 1 < count
        here = (lane >= STRIP * t) & (lane < STRIP * (t + 1))
        here_strip = jnp.where(here, jnp.where(lane == STRIP * t + sublane, one, zero), here_strip)
        if more:
            pick = lane == STRIP * (t + 1) + sublane
            next_strip = jnp.where(here, zero, strips[t + 1])
            next_cols = [single(next_strip, STRIP * (t + 1) + j) for j in span]
            sum_strip, sum_cols = None, [None] * STRIP
        for k in span:
            scale = lax.rsqrt(whole(cols[k], k))
            factor = cols[k] * scale
            for j in range(k + 1, STRIP):
                cols[j] = cols[j] - factor * whole(factor, j)
            row = whole(here_strip, k) * scale
            below = jnp.where(sublane > k, factor, zero)
            here_strip = jnp.where(sublane == k, row, here_strip - below * row)
            if more:
                across = jnp.sum(jnp.where(pick, row, zero), axis=1, keepdims=True)
                across = jnp.broadcast_to(across, (STRIP, BLK))
                terms = [across * row] + [across * whole(across, j) for j in span]
                if k == 0:
                    sum_strip, sum_cols = terms[0], terms[1:]
                elif k < STRIP - 1:
                    sum_strip = sum_strip + terms[0]
                    sum_cols = [p + q for p, q in zip(sum_cols, terms[1:])]
                else:
                    next_strip = (next_strip - sum_strip) - terms[0]
                    next_cols = [(b - p) - q for b, p, q in zip(next_cols, sum_cols, terms[1:])]
        solved.append(here_strip)
        if more:
            last_strip = here_strip
            here_strip, cols = next_strip, next_cols
        if t + 2 < count:
            change = dot_tn(last_strip, last_strip)
            for s in range(t + 2, count):
                strips[s] = jnp.where(here, zero, strips[s]) - change[STRIP * s:STRIP * (s + 1), :]
    return jnp.concatenate(
        [jnp.where(lane < STRIP * (t + 1), solved[t], zero) for t in range(count)], axis=0)


def halves(x):
    high = x.astype(BF16)
    return high, (x - high.astype(F32)).astype(BF16)


def dot_nt3(lhs, rhs):
    def one(p, q):
        return lax.dot_general(p, q, (((1,), (1,)), ((), ())), preferred_element_type=F32)
    return one(lhs[0], rhs[0]) + (one(lhs[0], rhs[1]) + one(lhs[1], rhs[0]))


def dot_nn3(lhs, rhs):
    def one(p, q):
        return jnp.dot(p, q, preferred_element_type=F32)
    return one(lhs[0], rhs[0]) + (one(lhs[0], rhs[1]) + one(lhs[1], rhs[0]))


(SPREAD0, SPREAD1, SPREAD2, HEAD_A, HEAD_B, ACROSS_A, ACROSS_B, PAIR_A, PAIR_B, ROWS, ROWS_PAIR,
 ROWS_ON, SWAP, FIRST_Z, FIRST_Y, THEN_Y, THEN_Z, TILES) = range(18)
TURNED = TILES + 8
ROWS_FAR = TURNED + 8
ROWS_FAR_ON = ROWS_FAR + 1
SEMS = ROWS_FAR + 2
L_SLAB, L_OWN, L_HEAD, L_ROWS, L_SWAP, L_IN, L_OUT, L_TURNED = 0, 1, 2, 3, 4, 5, 7, 9


def exchange_kernel(kr, out, panels, tiles, slab, head, work, diag, lower, whigh, wlow,
                    inbuf, high, low, obuf, turned, ssem, rsem, lsem):
    g = lax.axis_index("row")
    c = lax.axis_index("col")
    core = lax.rem(c, 2)
    other = (c // 2) * 2 + 1 - core
    y, z = g // 4, lax.rem(g, 4)
    swap_row = (g // 8) * 8 + c
    swap_col = lax.rem(g, 8)
    is_self = swap_col == c
    mine = pl.multiple_of(c * 64, 64)
    not_self = jnp.logical_not(is_self)
    chip = c // 2
    gives = chip == swap_col // 2

    def send(src, dst, index, row, col):
        pltpu.make_async_remote_copy(
            src_ref=src, dst_ref=dst, send_sem=ssem.at[index], recv_sem=rsem.at[index],
            device_id=(row, col), device_id_type=MESH).start()

    def local(src, dst, index):
        pltpu.make_async_copy(src, dst, lsem.at[index]).start()

    def done(ref, sem):
        pltpu.make_async_copy(ref, ref, sem).wait()

    local(kr.at[:, :, pl.ds(0, 1024)], slab, L_SLAB)
    for a in range(2):
        for b in range(4):
            at = pl.multiple_of((b * 8 + c) * 512, 512)
            local(kr.at[a, :, pl.ds(at, 512)], tiles.at[a * 4 + b, pl.ds(mine, 64), :], L_OWN)

    barrier = pltpu.get_barrier_semaphore()

    @pl.loop(1, 16)
    def _(o):
        pl.semaphore_signal(barrier, inc=1, device_id=(lax.rem(g + o, 16), c), device_id_type=MESH)

    @pl.loop(1, 8)
    def _(o):
        pl.semaphore_signal(barrier, inc=1, device_id=(g, lax.rem(c + o, 8)), device_id_type=MESH)

    @pl.when(not_self)
    def _():
        pl.semaphore_signal(barrier, inc=1, device_id=(swap_row, swap_col), device_id_type=MESH)

    for half in range(2):
        for o in range(2):
            src_row, src_col = c + 8 * half, chip * 2 + o

            @pl.when((src_row != g) | (src_col != c))
            def _():
                pl.semaphore_signal(barrier, inc=1, device_id=(src_row, src_col),
                                    device_id_type=MESH)

    pl.semaphore_wait(barrier, 22 + jnp.where(is_self, 15, 1 + jnp.where(gives, 16, 0)))

    done(slab, lsem.at[L_SLAB])

    def piece(which, q):
        return head.at[which, pl.ds(pl.multiple_of(mine + (q // 2) * 8, 8), 8),
                       pl.ds(pl.multiple_of(lax.rem(q, 2) * 256, 256), 256)]

    def spread(which, root, lanes_at, index):
        def src(q):
            return slab.at[0, pl.ds(pl.multiple_of((q // 2) * 8, 8), 8),
                           pl.ds(pl.multiple_of(lanes_at + lax.rem(q, 2) * 256, 256), 256)]

        @pl.when(g == root)
        def _():
            @pl.loop(1, 16)
            def _(o):
                q = lax.rem(g + o, 16)
                send(src(q), piece(which, q), index, q, c)
            local(src(g), piece(which, g), L_HEAD)

    spread(0, 0, 0, SPREAD0)
    spread(2, 1, 512, SPREAD2)
    spread(1, 0, 512, SPREAD1)

    def col_slab(a, r):
        return panels.at[2 + r // 8 + 2 * a, pl.ds(pl.multiple_of(lax.rem(r, 8) * 64, 64), 64), :]

    @pl.when(not_self)
    def _():
        for a in range(2):
            send(slab.at[a], col_slab(a, swap_row), SWAP, swap_row, swap_col)

    @pl.when(is_self)
    def _():
        for a in range(2):
            local(slab.at[a], col_slab(a, g), L_SWAP)

    def lanes(group):
        return pl.ds(pl.multiple_of(group * BLK, BLK), BLK)

    def send_parts(first, last):
        @pl.loop(first, last)
        def _(n):
            a, b = n // 4, lax.rem(n, 4)

            def whole(cc):
                at = pl.multiple_of((b * 8 + cc) * 512, 512)
                send(kr.at[a, :, pl.ds(at, 512)], tiles.at[n, pl.ds(mine, 64), :],
                     TILES + n, g, cc)

            whole(other)
            for k in range(2):
                whole(lax.rem(chip + 1, 4) * 2 + k)
                whole(lax.rem(chip + 3, 4) * 2 + k)
            there = lax.rem(chip + 2, 4)
            for k in range(2):
                for q in range(1, 4):
                    group = lax.rem(there + q, 4)
                    at = pl.multiple_of((b * 8 + there * 2 + k) * 512 + group * BLK, BLK)
                    send(kr.at[a, :, pl.ds(at, BLK)], tiles.at[n, pl.ds(mine, 64), lanes(group)],
                         TILES + n, g, there * 2 + k)

    def send_turned(first, last):
        far = lax.rem(swap_col // 2 + 2, 4)
        rows = pl.ds(pl.multiple_of(core * 64, 64), 64)

        @pl.when(gives)
        def _():
            @pl.loop(0, 16)
            def _(o):
                to = lax.rem(g + o, 16)
                away = (to != g) | not_self
                for dest_a in range(first, last):
                    for a in range(2):
                        n = dest_a * 4 + g // 8 + 2 * a
                        at = pl.multiple_of((dest_a * 16 + to) * 512 + far * BLK, BLK)
                        src = kr.at[a, :, pl.ds(at, BLK)]
                        dst = turned.at[n, rows, :]

                        @pl.when(away)
                        def _():
                            send(src, dst, TURNED + n, to, swap_col)

                        @pl.when(jnp.logical_not(away))
                        def _():
                            local(src, dst, L_TURNED)

    send_parts(0, 1)

    def gather_head(which, index):
        @pl.loop(1, 16)
        def _(o):
            send(piece(which, g), piece(which, g), index, lax.rem(g + o, 16), c)

    def chunk(which, col):
        return head.at[which, pl.ds(pl.multiple_of(col * 64, 64), 64), :]

    def across(which, index):
        for o in range(1, 4):
            send(chunk(which, c), chunk(which, c), index, g, lax.rem(c + 2 * o, 8))

    def pair(which, index):
        for o in range(4):
            src = chunk(which, lax.rem(c + 2 * o, 8))
            send(src, src, index, g, other)

    @pl.when(g == 0)
    def _():
        done(head.at[0, pl.ds(0, 16), pl.ds(0, 256)], lsem.at[L_HEAD])

    @pl.when(g == 1)
    def _():
        done(head.at[0, pl.ds(0, 8), pl.ds(0, 256)], lsem.at[L_HEAD])

    @pl.when(g != 0)
    def _():
        done(piece(0, g), rsem.at[SPREAD0])

    gather_head(0, HEAD_A)

    @pl.when(g != 0)
    def _():
        done(piece(1, g), rsem.at[SPREAD1])

    @pl.when(g != 1)
    def _():
        done(piece(2, g), rsem.at[SPREAD2])

    gather_head(1, HEAD_B)
    gather_head(2, HEAD_B)
    done(head.at[0, pl.ds(0, 120), pl.ds(0, 256)], rsem.at[HEAD_A])
    across(0, ACROSS_A)

    @pl.when(not_self)
    def _():
        done(slab, rsem.at[SWAP])

    @pl.when(is_self)
    def _():
        done(slab, lsem.at[L_SWAP])

    def row_of(dy, dz):
        return lax.rem(y + dy, 4) * 4 + lax.rem(z + dz, 4)

    for o in range(1, 4):
        send(col_slab(0, g), col_slab(0, g), FIRST_Z, row_of(0, o), c)
        send(col_slab(1, g), col_slab(1, g), FIRST_Y, row_of(o, 0), c)

    done(head.at[1, pl.ds(0, 240), pl.ds(0, 256)], rsem.at[HEAD_B])
    across(1, ACROSS_B)
    across(2, ACROSS_B)

    for a in range(2):
        dst = panels.at[a, pl.ds(mine, 64), :]
        for o in (1, 3):
            send(slab.at[a], dst, ROWS, g, lax.rem(c + 2 * o, 8))
        send(slab.at[a], dst, ROWS_PAIR, g, other)
        local(slab.at[a], dst, L_ROWS)

    send_parts(1, 4)
    done(head.at[0, pl.ds(0, 192), :], rsem.at[ACROSS_A])
    pair(0, PAIR_A)

    def second_stage():
        three = panels.at[0, pl.ds(0, 192), :]
        done(three, rsem.at[FIRST_Z])
        done(three, rsem.at[FIRST_Y])

        @pl.loop(0, 4)
        def _(n):
            from_z, from_y = row_of(0, n), row_of(n, 0)
            for o in range(1, 4):
                send(col_slab(0, from_z), col_slab(0, from_z), THEN_Y, row_of(o, 0), c)
                send(col_slab(1, from_y), col_slab(1, from_y), THEN_Z, row_of(0, o), c)

    def row_slab(a, o):
        at = pl.multiple_of(lax.rem(c + 2 * o, 8) * 64, 64)
        return panels.at[a, pl.ds(at, 64), :]

    def rows_on():
        done(panels.at[0, pl.ds(0, 256), :], rsem.at[ROWS])
        for a, o in ((0, 3), (1, 1)):
            send(row_slab(a, o), row_slab(a, o), ROWS_FAR, g, lax.rem(c + 8 - 2 * o, 8))
        for a in range(2):
            for o in (1, 3):
                send(row_slab(a, o), row_slab(a, o), ROWS_ON, g, other)
        send_parts(4, 8)

    def rows_far_on():
        done(panels.at[0, pl.ds(0, 128), :], rsem.at[ROWS_FAR])
        for a in range(2):
            send(row_slab(a, 2), row_slab(a, 2), ROWS_FAR_ON, g, other)

    def rows_done():
        done(panels.at[0, pl.ds(0, 128), :], rsem.at[ROWS_PAIR])
        done(panels.at[0, pl.ds(0, 256), :], rsem.at[ROWS_ON])
        done(panels.at[0, pl.ds(0, 128), :], rsem.at[ROWS_FAR_ON])
        done(slab, lsem.at[L_ROWS])

    done(head.at[0, pl.ds(0, 256), :], rsem.at[PAIR_A])

    lane_blk = lax.broadcasted_iota(jnp.int32, (BLK, 512), 1) // BLK
    blocks = 512 // BLK
    upper = (lax.broadcasted_iota(jnp.int32, (BLK, BLK), 0)
             <= lax.broadcasted_iota(jnp.int32, (BLK, BLK), 1))

    def factor(panel, between):
        @pl.loop(0, blocks)
        def _(kb):
            at = pl.multiple_of(kb * BLK, BLK)
            inverse = factor_block(work[pl.ds(at, BLK), pl.ds(at, BLK)])
            work[pl.ds(at, BLK), :] = jnp.dot(inverse, work[pl.ds(at, BLK), :], precision=HI,
                                              preferred_element_type=F32)
            diag[kb] = jnp.where(upper, work[pl.ds(at, BLK), pl.ds(at, BLK)], F32(0.0))
            work[pl.ds(at, BLK), pl.ds(at, BLK)] = inverse

            @pl.loop(kb + 1, blocks)
            def _(rb):
                to = pl.multiple_of(rb * BLK, BLK)
                change = dot_tn(work[pl.ds(at, BLK), pl.ds(to, BLK)], work[pl.ds(at, BLK), :])
                old = work[pl.ds(to, BLK), :]
                work[pl.ds(to, BLK), :] = jnp.where(lane_blk == kb, F32(0.0), old) - change

            between(kb)

        for r in range(blocks):
            here = slice(r * BLK, (r + 1) * BLK)
            row = jnp.where(lane_blk <= r, work[here, :], F32(0.0))
            whigh[2 * panel, here, :], wlow[2 * panel, here, :] = halves(row)
            for s in range(blocks):
                there = slice(s * BLK, (s + 1) * BLK)
                if s > r:
                    lower[2 * panel, here, there] = jnp.zeros((BLK, BLK), F32)
                elif s == r:
                    lower[2 * panel, here, there] = diag[r].T
                else:
                    lower[2 * panel, here, there] = work[there, here].T

    work[...] = head[0]

    def between(kb):
        @pl.when(kb == 0)
        def _():
            second_stage()

        @pl.when(kb == 1)
        def _():
            done(head.at[1, pl.ds(0, 384), :], rsem.at[ACROSS_B])
            pair(1, PAIR_B)
            pair(2, PAIR_B)

        @pl.when(kb == 2)
        def _():
            send_turned(0, 2)

        @pl.when(kb == 3)
        def _():
            rows_on()

    factor(0, between)
    done(head.at[pl.ds(1, 2), pl.ds(0, 256), :], rsem.at[PAIR_B])

    right = dot_nn3((whigh[0], wlow[0]), halves(head[1]))
    whigh[1], wlow[1] = halves(right)
    lower[1] = right.T
    work[...] = head[2] - dot_tn(right, right)
    factor(1, lambda kb: None)

    twelve = panels.at[pl.ds(0, 2), pl.ds(0, 384), :]

    def fetch(t, slot):
        return pltpu.make_async_copy(panels.at[t], inbuf.at[slot], lsem.at[L_IN + slot])

    done(twelve, rsem.at[THEN_Y])
    done(twelve, rsem.at[THEN_Z])
    fetch(2, 0).start()

    @pl.loop(0, 6)
    def _(step):
        t = lax.rem(step + 2, 6)
        slot = lax.rem(step, 2)

        @pl.when(step == 2)
        def _():
            rows_far_on()

        @pl.when(step == 3)
        def _():
            rows_done()

        @pl.when(step < 5)
        def _():
            fetch(lax.rem(step + 3, 6), 1 - slot).start()

        fetch(t, slot).wait()
        first = dot_nt3(halves(inbuf[slot, :, :512]), (whigh[0], wlow[0]))
        top, rest = halves(first)
        high[t, :, :512], low[t, :, :512] = top, rest
        left = inbuf[slot, :, 512:] - dot_nn3((top, rest), (whigh[1], wlow[1]))
        high[t, :, 512:], low[t, :, 512:] = halves(dot_nt3(halves(left), (whigh[2], wlow[2])))

    done(tiles.at[0], lsem.at[L_OWN])

    @pl.when(is_self)
    def _():
        done(tiles.at[0, pl.ds(0, 64), :], lsem.at[L_TURNED])

    def turn(n):
        own_source = is_self & (lax.rem(n, 2) == g // 8)

        @pl.when(own_source)
        def _():
            done(tiles.at[0, pl.ds(0, 16), :], rsem.at[TURNED + n])

        @pl.when(jnp.logical_not(own_source))
        def _():
            done(turned.at[n], rsem.at[TURNED + n])

        tiles[n, lanes(lax.rem(chip + 2, 4)), lanes(chip)] = turned[n].T

    def leave(pair_no, slot):
        at = pl.multiple_of(lax.rem(pair_no, 2) * 8, 8)
        return pltpu.make_async_copy(
            obuf.at[slot], out.at[pair_no // 2, :, pl.ds(at, 8), :], lsem.at[L_OUT + slot])

    @pl.loop(0, 8)
    def _(n):
        a, b = n // 4, lax.rem(n, 4)
        pair_no = n // 2
        slot = lax.rem(pair_no, 2)
        half = lax.rem(n, 2)
        flat = obuf.at[slot].reshape(512 * 8, 128)

        def put(value):
            for m in range(4):
                flat[pl.ds(half * 4 + m, 512, stride=8), :] = value[:, m * 128:(m + 1) * 128]

        @pl.when((half == 0) & (pair_no >= 2))
        def _():
            leave(pair_no - 2, slot).wait()

        done(tiles.at[n, pl.ds(0, 416), :], rsem.at[TILES + n])
        turn(n)
        special_row = (a == 0) & (g < 2)
        special_col = (b == 0) & (c < 2)

        @pl.when(jnp.logical_not(special_row | special_col))
        def _():
            put(tiles[n] - dot_nt3((high[a], low[a]), (high[2 + b], low[2 + b])))

        @pl.when(special_col & jnp.logical_not(special_row) & (c == 0))
        def _():
            put(high[a, :, :512].astype(F32) + low[a, :, :512].astype(F32))

        @pl.when(special_col & jnp.logical_not(special_row) & (c == 1))
        def _():
            put(high[a, :, 512:].astype(F32) + low[a, :, 512:].astype(F32))

        for corner in range(3):
            @pl.when(special_row & (b == 0) & (c <= g) & (g + c == corner))
            def _():
                put(lower[corner])

        @pl.when(special_row & ((b > 0) | (c > g)))
        def _():
            put(jnp.zeros((512, 512), F32))

        @pl.when(half == 1)
        def _():
            leave(pair_no, slot).start()

    for pair_no in range(2, 4):
        leave(pair_no, pair_no % 2).wait()

    @pl.loop(0, 8)
    def _(n):
        done(tiles.at[n, pl.ds(0, 416), :], ssem.at[TILES + n])

    for dest_a in range(0, 2):
        for a in range(2):
            index = TURNED + dest_a * 4 + g // 8 + 2 * a

            @pl.when(gives & not_self)
            def _():
                done(tiles.at[0, pl.ds(0, 256), :], ssem.at[index])

            @pl.when(is_self)
            def _():
                done(tiles.at[0, pl.ds(0, 240), :], ssem.at[index])

    @pl.when(g == 0)
    def _():
        done(head.at[0, pl.ds(0, 120), pl.ds(0, 256)], ssem.at[SPREAD0])
        done(head.at[0, pl.ds(0, 120), pl.ds(0, 256)], ssem.at[SPREAD1])

    @pl.when(g == 1)
    def _():
        done(head.at[0, pl.ds(0, 120), pl.ds(0, 256)], ssem.at[SPREAD2])

    done(head.at[0, pl.ds(0, 120), pl.ds(0, 256)], ssem.at[HEAD_A])
    done(head.at[1, pl.ds(0, 240), pl.ds(0, 256)], ssem.at[HEAD_B])
    done(head.at[0, pl.ds(0, 192), :], ssem.at[ACROSS_A])
    done(head.at[1, pl.ds(0, 384), :], ssem.at[ACROSS_B])
    done(head.at[0, pl.ds(0, 256), :], ssem.at[PAIR_A])
    done(head.at[pl.ds(1, 2), pl.ds(0, 256), :], ssem.at[PAIR_B])
    done(panels.at[0, pl.ds(0, 256), :], ssem.at[ROWS])
    done(panels.at[0, pl.ds(0, 128), :], ssem.at[ROWS_PAIR])
    done(panels.at[0, pl.ds(0, 256), :], ssem.at[ROWS_ON])
    done(panels.at[0, pl.ds(0, 128), :], ssem.at[ROWS_FAR])
    done(panels.at[0, pl.ds(0, 128), :], ssem.at[ROWS_FAR_ON])

    @pl.when(not_self)
    def _():
        done(slab, ssem.at[SWAP])

    three = panels.at[0, pl.ds(0, 192), :]
    done(three, ssem.at[FIRST_Z])
    done(three, ssem.at[FIRST_Y])
    done(twelve, ssem.at[THEN_Y])
    done(twelve, ssem.at[THEN_Z])


def exchange(rows):
    anyspace = pl.BlockSpec(memory_space=pl.ANY)
    return pl.pallas_call(
        exchange_kernel,
        out_shape=(
            jax.ShapeDtypeStruct((2, 512, 16, 128), F32),
            jax.ShapeDtypeStruct((6, 512, 1024), F32),
        ),
        in_specs=[anyspace],
        out_specs=(anyspace,) * 2,
        scratch_shapes=[
            pltpu.VMEM((8, 512, 512), F32),
            pltpu.VMEM((2, 64, 1024), F32),
            pltpu.VMEM((3, 512, 512), F32),
            pltpu.VMEM((512, 512), F32),
            pltpu.VMEM((4, BLK, BLK), F32),
            pltpu.VMEM((3, 512, 512), F32),
            pltpu.VMEM((3, 512, 512), BF16),
            pltpu.VMEM((3, 512, 512), BF16),
            pltpu.VMEM((2, 512, 1024), F32),
            pltpu.VMEM((6, 512, 1024), BF16),
            pltpu.VMEM((6, 512, 1024), BF16),
            pltpu.VMEM((2, 512, 8, 128), F32),
            pltpu.VMEM((8, BLK, BLK), F32),
            pltpu.SemaphoreType.DMA((SEMS,)),
            pltpu.SemaphoreType.DMA((SEMS,)),
            pltpu.SemaphoreType.DMA((10,)),
        ],
        compiler_params=pltpu.CompilerParams(
            collective_id=1, has_side_effects=True, vmem_limit_bytes=56 * 1024 * 1024),
        name="exchange",
    )(rows)


def place_kernel(src, dst, buf, sem):
    def take(i):
        return pltpu.make_async_copy(src.at[i // 4, pl.ds((i % 4) * 128, 128)], buf.at[i], sem.at[i])

    def put(i):
        return pltpu.make_async_copy(buf.at[i], dst.at[i // 4, pl.ds((i % 4) * 128, 128)],
                                     sem.at[8 + i])

    for i in range(8):
        take(i).start()
    for i in range(8):
        take(i).wait()
        put(i).start()
    for i in range(8):
        put(i).wait()


def place_result(values):
    anyspace = pl.BlockSpec(memory_space=pl.ANY)
    return pl.pallas_call(
        place_kernel,
        out_shape=jax.ShapeDtypeStruct((2, 512, 16, 128), F32),
        in_specs=[anyspace],
        out_specs=anyspace,
        scratch_shapes=[pltpu.VMEM((8, 128, 16, 128), F32), pltpu.SemaphoreType.DMA((16,))],
        compiler_params=pltpu.CompilerParams(vmem_limit_bytes=56 * 1024 * 1024),
        name="place",
    )(values)


def shards(kernel_rows):
    rows = kernel_rows.reshape(2, 64, 16384)
    out, _ = exchange(rows)
    return place_result(out).reshape(2, 1, 512, 4, 1, 512)


def solution(mesh):
    return jax.shard_map(
        shards,
        mesh=mesh,
        in_specs=(P(None, "row", "col", None, None),),
        out_specs=P(None, "row", None, None, "col", None),
        check_vma=False,
    )
```

```python
import functools
import jax
import jax.numpy as jnp
from jax import lax
from jax.experimental import pallas as pl
from jax.experimental.pallas import tpu as pltpu
from jax.sharding import PartitionSpec as P

MESH = pl.DeviceIdType.MESH
HI = lax.Precision.HIGHEST
F32 = jnp.float32
BF16 = jnp.bfloat16
BLK = 128
STRIP = 8


def dot_tn(lhs, rhs):
    return lax.dot_general(lhs, rhs, (((0,), (0,)), ((), ())), precision=HI,
                           preferred_element_type=F32)


def factor_block(block):
    count = BLK // STRIP
    lane = lax.broadcasted_iota(jnp.int32, (STRIP, BLK), 1)
    sublane = lax.broadcasted_iota(jnp.int32, (STRIP, BLK), 0)
    zero, one = F32(0.0), F32(1.0)
    span = range(STRIP)
    strips = [block[STRIP * t:STRIP * (t + 1), :] for t in range(count)]
    solved = []

    def whole(strip, i):
        return jnp.broadcast_to(strip[i:i + 1, :], (STRIP, BLK))

    def single(strip, at):
        return jnp.broadcast_to(strip[:, at:at + 1], (STRIP, BLK))

    here_strip = strips[0]
    cols = [single(here_strip, j) for j in span]
    for t in range(count):
        more = t + 1 < count
        here = (lane >= STRIP * t) & (lane < STRIP * (t + 1))
        here_strip = jnp.where(here, jnp.where(lane == STRIP * t + sublane, one, zero), here_strip)
        if more:
            pick = lane == STRIP * (t + 1) + sublane
            next_strip = jnp.where(here, zero, strips[t + 1])
            next_cols = [single(next_strip, STRIP * (t + 1) + j) for j in span]
            sum_strip, sum_cols = None, [None] * STRIP
        for k in span:
            scale = lax.rsqrt(whole(cols[k], k))
            factor = cols[k] * scale
            for j in range(k + 1, STRIP):
                cols[j] = cols[j] - factor * whole(factor, j)
            row = whole(here_strip, k) * scale
            below = jnp.where(sublane > k, factor, zero)
            here_strip = jnp.where(sublane == k, row, here_strip - below * row)
            if more:
                across = jnp.sum(jnp.where(pick, row, zero), axis=1, keepdims=True)
                across = jnp.broadcast_to(across, (STRIP, BLK))
                terms = [across * row] + [across * whole(across, j) for j in span]
                if k == 0:
                    sum_strip, sum_cols = terms[0], terms[1:]
                elif k < STRIP - 1:
                    sum_strip = sum_strip + terms[0]
                    sum_cols = [p + q for p, q in zip(sum_cols, terms[1:])]
                else:
                    next_strip = (next_strip - sum_strip) - terms[0]
                    next_cols = [(b - p) - q for b, p, q in zip(next_cols, sum_cols, terms[1:])]
        solved.append(here_strip)
        if more:
            last_strip = here_strip
            here_strip, cols = next_strip, next_cols
        if t + 2 < count:
            change = dot_tn(last_strip, last_strip)
            for s in range(t + 2, count):
                strips[s] = jnp.where(here, zero, strips[s]) - change[STRIP * s:STRIP * (s + 1), :]
    return jnp.concatenate(
        [jnp.where(lane < STRIP * (t + 1), solved[t], zero) for t in range(count)], axis=0)


def halves(x):
    high = x.astype(BF16)
    return high, (x - high.astype(F32)).astype(BF16)


def dot_nt3(lhs, rhs):
    def one(p, q):
        return lax.dot_general(p, q, (((1,), (1,)), ((), ())), preferred_element_type=F32)
    return one(lhs[0], rhs[0]) + (one(lhs[0], rhs[1]) + one(lhs[1], rhs[0]))


def dot_nn3(lhs, rhs):
    def one(p, q):
        return jnp.dot(p, q, preferred_element_type=F32)
    return one(lhs[0], rhs[0]) + (one(lhs[0], rhs[1]) + one(lhs[1], rhs[0]))


(SPREAD0, SPREAD1, SPREAD2, HEAD_A, HEAD_B, ACROSS_A, ACROSS_B, PAIR_A, PAIR_B, ROWS, ROWS_PAIR,
 ROWS_ON, SWAP, FIRST_Z, FIRST_Y, THEN_Y, THEN_Z, TILES) = range(18)
TURNED = TILES + 8
ROWS_FAR = TURNED + 8
ROWS_FAR_ON = ROWS_FAR + 1
SEMS = ROWS_FAR + 2
L_SLAB, L_OWN, L_HEAD, L_ROWS, L_SWAP, L_IN, L_OUT, L_TURNED = 0, 1, 2, 3, 4, 5, 7, 9


def exchange_kernel(kr, out, panels, tiles, slab, head, work, diag, lower, whigh, wlow,
                    inbuf, high, low, obuf, turned, ssem, rsem, lsem):
    g = lax.axis_index("row")
    c = lax.axis_index("col")
    core = lax.rem(c, 2)
    other = (c // 2) * 2 + 1 - core
    y, z = g // 4, lax.rem(g, 4)
    swap_row = (g // 8) * 8 + c
    swap_col = lax.rem(g, 8)
    is_self = swap_col == c
    mine = pl.multiple_of(c * 64, 64)
    not_self = jnp.logical_not(is_self)
    chip = c // 2
    gives = chip == swap_col // 2

    def send(src, dst, index, row, col):
        pltpu.make_async_remote_copy(
            src_ref=src, dst_ref=dst, send_sem=ssem.at[index], recv_sem=rsem.at[index],
            device_id=(row, col), device_id_type=MESH).start()

    def local(src, dst, index):
        pltpu.make_async_copy(src, dst, lsem.at[index]).start()

    def done(ref, sem):
        pltpu.make_async_copy(ref, ref, sem).wait()

    local(kr.at[:, :, pl.ds(0, 1024)], slab, L_SLAB)
    for a in range(2):
        for b in range(4):
            at = pl.multiple_of((b * 8 + c) * 512, 512)
            local(kr.at[a, :, pl.ds(at, 512)], tiles.at[a * 4 + b, pl.ds(mine, 64), :], L_OWN)

    barrier = pltpu.get_barrier_semaphore()

    @pl.loop(1, 16)
    def _(o):
        pl.semaphore_signal(barrier, inc=1, device_id=(lax.rem(g + o, 16), c), device_id_type=MESH)

    @pl.loop(1, 8)
    def _(o):
        pl.semaphore_signal(barrier, inc=1, device_id=(g, lax.rem(c + o, 8)), device_id_type=MESH)

    @pl.when(not_self)
    def _():
        pl.semaphore_signal(barrier, inc=1, device_id=(swap_row, swap_col), device_id_type=MESH)

    for half in range(2):
        for o in range(2):
            src_row, src_col = c + 8 * half, chip * 2 + o

            @pl.when((src_row != g) | (src_col != c))
            def _():
                pl.semaphore_signal(barrier, inc=1, device_id=(src_row, src_col),
                                    device_id_type=MESH)

    pl.semaphore_wait(barrier, 22 + jnp.where(is_self, 15, 1 + jnp.where(gives, 16, 0)))

    done(slab, lsem.at[L_SLAB])

    def piece(which, q):
        return head.at[which, pl.ds(pl.multiple_of(mine + (q // 2) * 8, 8), 8),
                       pl.ds(pl.multiple_of(lax.rem(q, 2) * 256, 256), 256)]

    def spread(which, root, lanes_at, index):
        def src(q):
            return slab.at[0, pl.ds(pl.multiple_of((q // 2) * 8, 8), 8),
                           pl.ds(pl.multiple_of(lanes_at + lax.rem(q, 2) * 256, 256), 256)]

        @pl.when(g == root)
        def _():
            @pl.loop(1, 16)
            def _(o):
                q = lax.rem(g + o, 16)
                send(src(q), piece(which, q), index, q, c)
            local(src(g), piece(which, g), L_HEAD)

    spread(0, 0, 0, SPREAD0)
    spread(2, 1, 512, SPREAD2)
    spread(1, 0, 512, SPREAD1)

    def col_slab(a, r):
        return panels.at[2 + r // 8 + 2 * a, pl.ds(pl.multiple_of(lax.rem(r, 8) * 64, 64), 64), :]

    @pl.when(not_self)
    def _():
        for a in range(2):
            send(slab.at[a], col_slab(a, swap_row), SWAP, swap_row, swap_col)

    @pl.when(is_self)
    def _():
        for a in range(2):
            local(slab.at[a], col_slab(a, g), L_SWAP)

    def lanes(group):
        return pl.ds(pl.multiple_of(group * BLK, BLK), BLK)

    def send_parts(first, last):
        @pl.loop(first, last)
        def _(n):
            a, b = n // 4, lax.rem(n, 4)

            def whole(cc):
                at = pl.multiple_of((b * 8 + cc) * 512, 512)
                send(kr.at[a, :, pl.ds(at, 512)], tiles.at[n, pl.ds(mine, 64), :],
                     TILES + n, g, cc)

            whole(other)
            for k in range(2):
                whole(lax.rem(chip + 1, 4) * 2 + k)
                whole(lax.rem(chip + 3, 4) * 2 + k)
            there = lax.rem(chip + 2, 4)
            for k in range(2):
                for q in range(1, 4):
                    group = lax.rem(there + q, 4)
                    at = pl.multiple_of((b * 8 + there * 2 + k) * 512 + group * BLK, BLK)
                    send(kr.at[a, :, pl.ds(at, BLK)], tiles.at[n, pl.ds(mine, 64), lanes(group)],
                         TILES + n, g, there * 2 + k)

    def send_turned(first, last):
        far = lax.rem(swap_col // 2 + 2, 4)
        rows = pl.ds(pl.multiple_of(core * 64, 64), 64)

        @pl.when(gives)
        def _():
            @pl.loop(0, 16)
            def _(o):
                to = lax.rem(g + o, 16)
                away = (to != g) | not_self
                for dest_a in range(first, last):
                    for a in range(2):
                        n = dest_a * 4 + g // 8 + 2 * a
                        at = pl.multiple_of((dest_a * 16 + to) * 512 + far * BLK, BLK)
                        src = kr.at[a, :, pl.ds(at, BLK)]
                        dst = turned.at[n, rows, :]

                        @pl.when(away)
                        def _():
                            send(src, dst, TURNED + n, to, swap_col)

                        @pl.when(jnp.logical_not(away))
                        def _():
                            local(src, dst, L_TURNED)

    send_parts(0, 1)

    def gather_head(which, index):
        @pl.loop(1, 16)
        def _(o):
            send(piece(which, g), piece(which, g), index, lax.rem(g + o, 16), c)

    def chunk(which, col):
        return head.at[which, pl.ds(pl.multiple_of(col * 64, 64), 64), :]

    def across(which, index):
        for o in range(1, 4):
            send(chunk(which, c), chunk(which, c), index, g, lax.rem(c + 2 * o, 8))

    def pair(which, index):
        for o in range(4):
            src = chunk(which, lax.rem(c + 2 * o, 8))
            send(src, src, index, g, other)

    @pl.when(g == 0)
    def _():
        done(head.at[0, pl.ds(0, 16), pl.ds(0, 256)], lsem.at[L_HEAD])

    @pl.when(g == 1)
    def _():
        done(head.at[0, pl.ds(0, 8), pl.ds(0, 256)], lsem.at[L_HEAD])

    @pl.when(g != 0)
    def _():
        done(piece(0, g), rsem.at[SPREAD0])

    gather_head(0, HEAD_A)

    @pl.when(g != 0)
    def _():
        done(piece(1, g), rsem.at[SPREAD1])

    @pl.when(g != 1)
    def _():
        done(piece(2, g), rsem.at[SPREAD2])

    gather_head(1, HEAD_B)
    gather_head(2, HEAD_B)
    done(head.at[0, pl.ds(0, 120), pl.ds(0, 256)], rsem.at[HEAD_A])
    across(0, ACROSS_A)

    @pl.when(not_self)
    def _():
        done(slab, rsem.at[SWAP])

    @pl.when(is_self)
    def _():
        done(slab, lsem.at[L_SWAP])

    def row_of(dy, dz):
        return lax.rem(y + dy, 4) * 4 + lax.rem(z + dz, 4)

    for o in range(1, 4):
        send(col_slab(0, g), col_slab(0, g), FIRST_Z, row_of(0, o), c)
        send(col_slab(1, g), col_slab(1, g), FIRST_Y, row_of(o, 0), c)

    done(head.at[1, pl.ds(0, 240), pl.ds(0, 256)], rsem.at[HEAD_B])
    across(1, ACROSS_B)
    across(2, ACROSS_B)

    for a in range(2):
        dst = panels.at[a, pl.ds(mine, 64), :]
        for o in (1, 3):
            send(slab.at[a], dst, ROWS, g, lax.rem(c + 2 * o, 8))
        send(slab.at[a], dst, ROWS_PAIR, g, other)
        local(slab.at[a], dst, L_ROWS)

    send_parts(1, 4)
    done(head.at[0, pl.ds(0, 192), :], rsem.at[ACROSS_A])
    pair(0, PAIR_A)

    def second_stage():
        three = panels.at[0, pl.ds(0, 192), :]
        done(three, rsem.at[FIRST_Z])
        done(three, rsem.at[FIRST_Y])

        @pl.loop(0, 4)
        def _(n):
            from_z, from_y = row_of(0, n), row_of(n, 0)
            for o in range(1, 4):
                send(col_slab(0, from_z), col_slab(0, from_z), THEN_Y, row_of(o, 0), c)
                send(col_slab(1, from_y), col_slab(1, from_y), THEN_Z, row_of(0, o), c)

    def row_slab(a, o):
        at = pl.multiple_of(lax.rem(c + 2 * o, 8) * 64, 64)
        return panels.at[a, pl.ds(at, 64), :]

    def rows_on():
        done(panels.at[0, pl.ds(0, 256), :], rsem.at[ROWS])
        for a, o in ((0, 3), (1, 1)):
            send(row_slab(a, o), row_slab(a, o), ROWS_FAR, g, lax.rem(c + 8 - 2 * o, 8))
        for a in range(2):
            for o in (1, 3):
                send(row_slab(a, o), row_slab(a, o), ROWS_ON, g, other)
        send_parts(4, 8)

    def rows_far_on():
        done(panels.at[0, pl.ds(0, 128), :], rsem.at[ROWS_FAR])
        for a in range(2):
            send(row_slab(a, 2), row_slab(a, 2), ROWS_FAR_ON, g, other)

    def rows_done():
        done(panels.at[0, pl.ds(0, 128), :], rsem.at[ROWS_PAIR])
        done(panels.at[0, pl.ds(0, 256), :], rsem.at[ROWS_ON])
        done(panels.at[0, pl.ds(0, 128), :], rsem.at[ROWS_FAR_ON])
        done(slab, lsem.at[L_ROWS])

    done(head.at[0, pl.ds(0, 256), :], rsem.at[PAIR_A])

    lane_blk = lax.broadcasted_iota(jnp.int32, (BLK, 512), 1) // BLK
    blocks = 512 // BLK
    upper = (lax.broadcasted_iota(jnp.int32, (BLK, BLK), 0)
             <= lax.broadcasted_iota(jnp.int32, (BLK, BLK), 1))

    def factor(panel, between):
        @pl.loop(0, blocks)
        def _(kb):
            at = pl.multiple_of(kb * BLK, BLK)
            inverse = factor_block(work[pl.ds(at, BLK), pl.ds(at, BLK)])
            work[pl.ds(at, BLK), :] = jnp.dot(inverse, work[pl.ds(at, BLK), :], precision=HI,
                                              preferred_element_type=F32)
            diag[kb] = jnp.where(upper, work[pl.ds(at, BLK), pl.ds(at, BLK)], F32(0.0))
            work[pl.ds(at, BLK), pl.ds(at, BLK)] = inverse

            @pl.loop(kb + 1, blocks)
            def _(rb):
                to = pl.multiple_of(rb * BLK, BLK)
                change = dot_tn(work[pl.ds(at, BLK), pl.ds(to, BLK)], work[pl.ds(at, BLK), :])
                old = work[pl.ds(to, BLK), :]
                work[pl.ds(to, BLK), :] = jnp.where(lane_blk == kb, F32(0.0), old) - change

            between(kb)

        for r in range(blocks):
            here = slice(r * BLK, (r + 1) * BLK)
            row = jnp.where(lane_blk <= r, work[here, :], F32(0.0))
            whigh[2 * panel, here, :], wlow[2 * panel, here, :] = halves(row)
            for s in range(blocks):
                there = slice(s * BLK, (s + 1) * BLK)
                if s > r:
                    lower[2 * panel, here, there] = jnp.zeros((BLK, BLK), F32)
                elif s == r:
                    lower[2 * panel, here, there] = diag[r].T
                else:
                    lower[2 * panel, here, there] = work[there, here].T

    work[...] = head[0]

    def between(kb):
        @pl.when(kb == 0)
        def _():
            second_stage()

        @pl.when(kb == 1)
        def _():
            done(head.at[1, pl.ds(0, 384), :], rsem.at[ACROSS_B])
            pair(1, PAIR_B)
            pair(2, PAIR_B)

        @pl.when(kb == 2)
        def _():
            send_turned(0, 2)

        @pl.when(kb == 3)
        def _():
            rows_on()

    factor(0, between)
    done(head.at[pl.ds(1, 2), pl.ds(0, 256), :], rsem.at[PAIR_B])

    right = dot_nn3((whigh[0], wlow[0]), halves(head[1]))
    whigh[1], wlow[1] = halves(right)
    lower[1] = right.T
    work[...] = head[2] - dot_tn(right, right)
    factor(1, lambda kb: None)

    twelve = panels.at[pl.ds(0, 2), pl.ds(0, 384), :]

    def fetch(t, slot):
        return pltpu.make_async_copy(panels.at[t], inbuf.at[slot], lsem.at[L_IN + slot])

    done(twelve, rsem.at[THEN_Y])
    done(twelve, rsem.at[THEN_Z])
    fetch(2, 0).start()

    @pl.loop(0, 6)
    def _(step):
        t = lax.rem(step + 2, 6)
        slot = lax.rem(step, 2)

        @pl.when(step == 2)
        def _():
            rows_far_on()

        @pl.when(step == 3)
        def _():
            rows_done()

        @pl.when(step < 5)
        def _():
            fetch(lax.rem(step + 3, 6), 1 - slot).start()

        fetch(t, slot).wait()
        first = dot_nt3(halves(inbuf[slot, :, :512]), (whigh[0], wlow[0]))
        top, rest = halves(first)
        high[t, :, :512], low[t, :, :512] = top, rest
        left = inbuf[slot, :, 512:] - dot_nn3((top, rest), (whigh[1], wlow[1]))
        high[t, :, 512:], low[t, :, 512:] = halves(dot_nt3(halves(left), (whigh[2], wlow[2])))

    done(tiles.at[0], lsem.at[L_OWN])

    @pl.when(is_self)
    def _():
        done(tiles.at[0, pl.ds(0, 64), :], lsem.at[L_TURNED])

    def turn(n):
        own_source = is_self & (lax.rem(n, 2) == g // 8)

        @pl.when(own_source)
        def _():
            done(tiles.at[0, pl.ds(0, 16), :], rsem.at[TURNED + n])

        @pl.when(jnp.logical_not(own_source))
        def _():
            done(turned.at[n], rsem.at[TURNED + n])

        tiles[n, lanes(lax.rem(chip + 2, 4)), lanes(chip)] = turned[n].T

    def leave(pair_no, slot):
        at = pl.multiple_of(lax.rem(pair_no, 2) * 8, 8)
        return pltpu.make_async_copy(
            obuf.at[slot], out.at[pair_no // 2, :, pl.ds(at, 8), :], lsem.at[L_OUT + slot])

    @pl.loop(0, 8)
    def _(n):
        a, b = n // 4, lax.rem(n, 4)
        pair_no = n // 2
        slot = lax.rem(pair_no, 2)
        half = lax.rem(n, 2)
        flat = obuf.at[slot].reshape(512 * 8, 128)

        def put(value):
            for m in range(4):
                flat[pl.ds(half * 4 + m, 512, stride=8), :] = value[:, m * 128:(m + 1) * 128]

        @pl.when((half == 0) & (pair_no >= 2))
        def _():
            leave(pair_no - 2, slot).wait()

        special_row = (a == 0) & (g < 2)
        special_col = (b == 0) & (c < 2)
        plain = jnp.logical_not(special_row | special_col)

        @pl.when(plain)
        def _():
            work[...] = dot_nt3((high[a], low[a]), (high[2 + b], low[2 + b]))

        done(tiles.at[n, pl.ds(0, 416), :], rsem.at[TILES + n])
        turn(n)

        @pl.when(plain)
        def _():
            put(tiles[n] - work[...])

        @pl.when(special_col & jnp.logical_not(special_row) & (c == 0))
        def _():
            put(high[a, :, :512].astype(F32) + low[a, :, :512].astype(F32))

        @pl.when(special_col & jnp.logical_not(special_row) & (c == 1))
        def _():
            put(high[a, :, 512:].astype(F32) + low[a, :, 512:].astype(F32))

        for corner in range(3):
            @pl.when(special_row & (b == 0) & (c <= g) & (g + c == corner))
            def _():
                put(lower[corner])

        @pl.when(special_row & ((b > 0) | (c > g)))
        def _():
            put(jnp.zeros((512, 512), F32))

        @pl.when(half == 1)
        def _():
            leave(pair_no, slot).start()

    for pair_no in range(2, 4):
        leave(pair_no, pair_no % 2).wait()

    @pl.loop(0, 8)
    def _(n):
        done(tiles.at[n, pl.ds(0, 416), :], ssem.at[TILES + n])

    for dest_a in range(0, 2):
        for a in range(2):
            index = TURNED + dest_a * 4 + g // 8 + 2 * a

            @pl.when(gives & not_self)
            def _():
                done(tiles.at[0, pl.ds(0, 256), :], ssem.at[index])

            @pl.when(is_self)
            def _():
                done(tiles.at[0, pl.ds(0, 240), :], ssem.at[index])

    @pl.when(g == 0)
    def _():
        done(head.at[0, pl.ds(0, 120), pl.ds(0, 256)], ssem.at[SPREAD0])
        done(head.at[0, pl.ds(0, 120), pl.ds(0, 256)], ssem.at[SPREAD1])

    @pl.when(g == 1)
    def _():
        done(head.at[0, pl.ds(0, 120), pl.ds(0, 256)], ssem.at[SPREAD2])

    done(head.at[0, pl.ds(0, 120), pl.ds(0, 256)], ssem.at[HEAD_A])
    done(head.at[1, pl.ds(0, 240), pl.ds(0, 256)], ssem.at[HEAD_B])
    done(head.at[0, pl.ds(0, 192), :], ssem.at[ACROSS_A])
    done(head.at[1, pl.ds(0, 384), :], ssem.at[ACROSS_B])
    done(head.at[0, pl.ds(0, 256), :], ssem.at[PAIR_A])
    done(head.at[pl.ds(1, 2), pl.ds(0, 256), :], ssem.at[PAIR_B])
    done(panels.at[0, pl.ds(0, 256), :], ssem.at[ROWS])
    done(panels.at[0, pl.ds(0, 128), :], ssem.at[ROWS_PAIR])
    done(panels.at[0, pl.ds(0, 256), :], ssem.at[ROWS_ON])
    done(panels.at[0, pl.ds(0, 128), :], ssem.at[ROWS_FAR])
    done(panels.at[0, pl.ds(0, 128), :], ssem.at[ROWS_FAR_ON])

    @pl.when(not_self)
    def _():
        done(slab, ssem.at[SWAP])

    three = panels.at[0, pl.ds(0, 192), :]
    done(three, ssem.at[FIRST_Z])
    done(three, ssem.at[FIRST_Y])
    done(twelve, ssem.at[THEN_Y])
    done(twelve, ssem.at[THEN_Z])


def exchange(rows):
    anyspace = pl.BlockSpec(memory_space=pl.ANY)
    return pl.pallas_call(
        exchange_kernel,
        out_shape=(
            jax.ShapeDtypeStruct((2, 512, 16, 128), F32),
            jax.ShapeDtypeStruct((6, 512, 1024), F32),
        ),
        in_specs=[anyspace],
        out_specs=(anyspace,) * 2,
        scratch_shapes=[
            pltpu.VMEM((8, 512, 512), F32),
            pltpu.VMEM((2, 64, 1024), F32),
            pltpu.VMEM((3, 512, 512), F32),
            pltpu.VMEM((512, 512), F32),
            pltpu.VMEM((4, BLK, BLK), F32),
            pltpu.VMEM((3, 512, 512), F32),
            pltpu.VMEM((3, 512, 512), BF16),
            pltpu.VMEM((3, 512, 512), BF16),
            pltpu.VMEM((2, 512, 1024), F32),
            pltpu.VMEM((6, 512, 1024), BF16),
            pltpu.VMEM((6, 512, 1024), BF16),
            pltpu.VMEM((2, 512, 8, 128), F32),
            pltpu.VMEM((8, BLK, BLK), F32),
            pltpu.SemaphoreType.DMA((SEMS,)),
            pltpu.SemaphoreType.DMA((SEMS,)),
            pltpu.SemaphoreType.DMA((10,)),
        ],
        compiler_params=pltpu.CompilerParams(
            collective_id=1, has_side_effects=True, vmem_limit_bytes=56 * 1024 * 1024),
        name="exchange",
    )(rows)


def place_kernel(src, dst, buf, sem):
    def take(i):
        return pltpu.make_async_copy(src.at[i // 4, pl.ds((i % 4) * 128, 128)], buf.at[i], sem.at[i])

    def put(i):
        return pltpu.make_async_copy(buf.at[i], dst.at[i // 4, pl.ds((i % 4) * 128, 128)],
                                     sem.at[8 + i])

    for i in range(8):
        take(i).start()
    for i in range(8):
        take(i).wait()
        put(i).start()
    for i in range(8):
        put(i).wait()


def place_result(values):
    anyspace = pl.BlockSpec(memory_space=pl.ANY)
    return pl.pallas_call(
        place_kernel,
        out_shape=jax.ShapeDtypeStruct((2, 512, 16, 128), F32),
        in_specs=[anyspace],
        out_specs=anyspace,
        scratch_shapes=[pltpu.VMEM((8, 128, 16, 128), F32), pltpu.SemaphoreType.DMA((16,))],
        compiler_params=pltpu.CompilerParams(vmem_limit_bytes=56 * 1024 * 1024),
        name="place",
    )(values)


def shards(kernel_rows):
    rows = kernel_rows.reshape(2, 64, 16384)
    out, _ = exchange(rows)
    return place_result(out).reshape(2, 1, 512, 4, 1, 512)


def solution(mesh):
    return jax.shard_map(
        shards,
        mesh=mesh,
        in_specs=(P(None, "row", "col", None, None),),
        out_specs=P(None, "row", None, None, "col", None),
        check_vma=False,
    )
```
